512 devices in a mesh: gx: 32 (over y_lo, z), gy: 16 (over x, y_hi, core).
Axes of the slice: x: 4, y: 4 (y_hi: 2, y_lo: 2; y = y_hi * 2 + y_lo), z: 16, core: 2. Of those that a mesh axis runs over, the one named last changes fastest.
Arguments:
- mass_per_volume: float32 [256, 512, 128], P('gx', 'gy'), may hold values from 0.5 to 2
- momentum: float32 [3, 256, 512, 128], P(None, 'gx', 'gy'), may hold values from -0.9 to 0.9
- energy: float32 [256, 512, 128], P('gx', 'gy'), may hold values from 3 to 8
Outputs:
- tendency: float32 [5, 256, 512, 128], P(None, 'gx', 'gy')
- advanced: float32 [5, 256, 512, 128], P(None, 'gx', 'gy')
The draws below stay inside these ranges and needn't reach their ends.
All inputs are finite; a program needn't handle non-finite values.
Results may differ from the reference program's by a relative error of at most 0.00016.
Values sent between devices are 32-bit elements; how exact they have to be, the bound alone decides.
A program may use at most 64 MiB of HBM per device.

```python
import math
import jax
import jax.numpy as jnp
import numpy as np
from jax import lax

CX = 8
CY = 8
NZ = 512
HALO = 4
NX = 256
NY = 128


def shard_levels(own_key, dims, shards, low, top_value):
    loudness, own = 1.0, jax.random.fold_in(own_key, 6)
    for dim, shards_of in shards:
        heights = jnp.exp(jax.random.uniform(jax.random.fold_in(own, dim), (shards_of,), jnp.float32, low / len(shards), top_value / len(shards)))
        loudness = loudness * jnp.repeat(heights, dims[dim] // shards_of).reshape([-1 if axis == dim else 1 for axis in range(len(dims))])
    return loudness


def setup_inputs(seed: int = 0) -> dict:
    seeds = jax.random.split(jax.random.key(seed), 4)
    mass_per_volume = jnp.clip(jnp.exp(math.log(2.0) - 1.3862944 * jax.random.uniform(seeds[0], (NX, NZ, NY), jnp.float32) ** shard_levels(seeds[0], (NX, NZ, NY), ((0, 32), (1, 16)), -0.2, 0.2)), 0.5, 2.0)
    momentum = jnp.clip(jax.random.uniform(seeds[1], (3, NX, NZ, NY), jnp.float32, -0.9, 0.9) * shard_levels(seeds[1], (3, NX, NZ, NY), ((1, 32), (2, 16)), -0.4, 0.0), -0.9, 0.9)
    energy = jnp.clip(jnp.exp(math.log(8.0) - 0.98082925 * jax.random.uniform(seeds[2], (NX, NZ, NY), jnp.float32) ** shard_levels(seeds[2], (NX, NZ, NY), ((0, 32), (1, 16)), -0.2, 0.2)), 3.0, 8.0)
    return dict(mass_per_volume=mass_per_volume, momentum=momentum, energy=energy)


heat_ratio = 1.4
shear_resistance_reference = 0.08
sutherland_power_law = 0.7
prandtl = 0.72
section_step = 0.05
compact_alpha = 1.0 / 3.0
compact_near = 14.0 / 9.0
compact_far = 1.0 / 9.0


def tridiagonal_inverse_product(length, stencil):
    solved = np.array(stencil)
    upper_ratio = np.zeros(length)
    for row_index in range(length):
        if row_index == 0:
            pivot_value = 1.0
            solved[row_index] = solved[row_index] / pivot_value
        else:
            pivot_value = 1.0 - compact_alpha * upper_ratio[row_index - 1]
            solved[row_index] = (solved[row_index] - compact_alpha * solved[row_index - 1]) / pivot_value
        upper_ratio[row_index] = compact_alpha / pivot_value
    for row_index in range(length - 2, -1, -1):
        solved[row_index] = solved[row_index] - upper_ratio[row_index] * solved[row_index + 1]
    return solved


def compact_matrix(block_size, margin):
    length = block_size + 2 * margin
    stencil = (compact_near / 2.0) * (np.eye(length, k=1) - np.eye(length, k=-1))
    stencil = stencil + (compact_far / 4.0) * (np.eye(length, k=2) - np.eye(length, k=-2))
    inverse_product = tridiagonal_inverse_product(length, stencil)
    return inverse_product[margin:margin + block_size].astype(np.float32)


def right_side(conserved, gradients_of, derive_x, derive_y, derive_z):
    mass_per_volume = conserved[0]
    momentum = conserved[1:4]
    energy = conserved[4]
    local_speed_vector = momentum / mass_per_volume
    kinetic = 0.5 * jnp.sum(momentum * local_speed_vector, axis=0)
    normal_force_per_area = (heat_ratio - 1.0) * (energy - kinetic)
    thermal_state = normal_force_per_area / mass_per_volume
    basic_quantities = jnp.concatenate([local_speed_vector, thermal_state[None]], 0)
    gradients = gradients_of(basic_quantities)
    shear_resistance = shear_resistance_reference * jnp.power(thermal_state, sutherland_power_law)
    conductivity = shear_resistance * heat_ratio / ((heat_ratio - 1.0) * prandtl)
    dilatation = gradients[0][0] + gradients[1][1] + gradients[2][2]
    derivers = (derive_x, derive_y, derive_z)
    accumulated = None
    for direction in range(3):
        stress_column = [shear_resistance * (gradients[direction][component] + gradients[component][direction]) for component in range(3)]
        stress_column[direction] = stress_column[direction] - (2.0 / 3.0) * shear_resistance * dilatation
        fluxes = [momentum[direction]]
        for component in range(3):
            moment_flux = momentum[component] * local_speed_vector[direction] - stress_column[component]
            if component == direction:
                moment_flux = moment_flux + normal_force_per_area
            fluxes.append(moment_flux)
        work_term = stress_column[0] * local_speed_vector[0] + stress_column[1] * local_speed_vector[1] + stress_column[2] * local_speed_vector[2]
        fluxes.append((energy + normal_force_per_area) * local_speed_vector[direction] - work_term - conductivity * gradients[direction][3])
        divergence_part = derivers[direction](jnp.stack(fluxes))
        accumulated = divergence_part if accumulated is None else accumulated + divergence_part
    return -accumulated


def along_blocks(values, axis_pos, block_size):
    matrix = jnp.asarray(compact_matrix(block_size, HALO), jnp.float32)
    rotated = jnp.moveaxis(values, axis_pos, 0)
    total = rotated.shape[0]
    padded = jnp.concatenate([rotated[total - HALO:], rotated, rotated[:HALO]], 0)
    positions = (np.arange(total // block_size)[:, None] * block_size + np.arange(block_size + 2 * HALO)[None, :]).astype(np.int32)
    segments = padded[positions]
    result = jnp.einsum("il,bl...->bi...", matrix, segments, precision=lax.Precision.HIGHEST)
    return jnp.moveaxis(result.reshape(rotated.shape), 0, axis_pos)


def along_span(values, axis_pos):
    total = values.shape[axis_pos]
    spectra = jnp.fft.rfft(values, axis=axis_pos)
    wavenumbers = 2.0 * np.pi * np.arange(total // 2 + 1) / total
    wavenumbers[-1] = 0.0
    shape_b = [1] * values.ndim
    shape_b[axis_pos] = total // 2 + 1
    factor = jnp.asarray(wavenumbers.reshape(shape_b), jnp.float32)
    return jnp.fft.irfft(spectra * (1j * factor), n=total, axis=axis_pos)


def per_component(function, stacked):
    return jnp.stack([function(stacked[position]) for position in range(stacked.shape[0])])


def derive_x(stacked):
    return per_component(lambda single: along_blocks(single, 0, CX), stacked)


def derive_y(stacked):
    return per_component(lambda single: along_blocks(single, 2, CY), stacked)


def derive_z(stacked):
    return per_component(lambda single: along_span(single, 1), stacked)


def gradients_all(basic_quantities):
    return (derive_x(basic_quantities), derive_y(basic_quantities), derive_z(basic_quantities))


def reference(mass_per_volume, momentum, energy):
    conserved = jnp.concatenate([mass_per_volume[None], momentum, energy[None]], 0)
    tendency = right_side(conserved, gradients_all, derive_x, derive_y, derive_z)
    return tendency, conserved + section_step * tendency
```

```python
import jax
import jax.numpy as jnp
import ml_dtypes
import numpy as np
from jax import lax
from jax.experimental import pallas as pl
from jax.experimental.pallas import tpu as pltpu
from jax.sharding import PartitionSpec as P

CX = 8
CY = 8
NZ = 512
NY = 128
HALO = 4
GY = 16
ZB = NZ // GY
HZ = ZB // 2
MESH = pl.DeviceIdType.MESH

heat_ratio = 1.4
shear_resistance_reference = 0.08
sutherland_power_law = 0.7
prandtl = 0.72
section_step = 0.05
compact_alpha = 1.0 / 3.0
compact_near = 14.0 / 9.0
compact_far = 1.0 / 9.0
conduction = heat_ratio / ((heat_ratio - 1.0) * prandtl)


def tridiagonal_inverse_product(length, stencil):
    solved = np.array(stencil)
    upper_ratio = np.zeros(length)
    for row_index in range(length):
        if row_index == 0:
            pivot_value = 1.0
            solved[row_index] = solved[row_index] / pivot_value
        else:
            pivot_value = 1.0 - compact_alpha * upper_ratio[row_index - 1]
            solved[row_index] = (
                solved[row_index] - compact_alpha * solved[row_index - 1]
            ) / pivot_value
        upper_ratio[row_index] = compact_alpha / pivot_value
    for row_index in range(length - 2, -1, -1):
        solved[row_index] = solved[row_index] - upper_ratio[row_index] * solved[row_index + 1]
    return solved


def compact_matrix(block_size, margin):
    length = block_size + 2 * margin
    stencil = compact_near / 2.0 * (np.eye(length, k=1) - np.eye(length, k=-1))
    stencil = stencil + compact_far / 4.0 * (np.eye(length, k=2) - np.eye(length, k=-2))
    inverse_product = tridiagonal_inverse_product(length, stencil)
    return inverse_product[margin : margin + block_size]


def pitch_matrix(total, block_size):
    matrix = compact_matrix(block_size, HALO)
    result = np.zeros((total, total))
    rows_all = np.arange(total)
    block_start = rows_all // block_size * block_size
    for offset in range(block_size + 2 * HALO):
        columns = (block_start - HALO + offset) % total
        result[rows_all, columns] += matrix[rows_all % block_size, offset]
    return result


def span_kernel(offsets, total):
    angles = np.pi * offsets / total
    signs = np.where(offsets % 2 == 0, 1.0, -1.0)
    zero = offsets % total == 0
    sines = np.where(zero, 1.0, np.sin(angles))
    return np.where(zero, 0.0, np.pi / total * signs * np.cos(angles) / sines)


def high_low(matrix):
    high = matrix.astype(ml_dtypes.bfloat16)
    low = (matrix - high.astype(np.float64)).astype(ml_dtypes.bfloat16)
    return high, low


def span_operand():
    z = (np.arange(GY)[:, None] * ZB + np.arange(HZ)[None, :]).reshape(-1)
    near = span_kernel(z[:, None] - z[None, :], NZ)
    far = span_kernel(z[:, None] - (z[None, :] + HZ), NZ)
    return high_low(np.concatenate([near, far], 1))


def pitch_operand():
    high, low = high_low(pitch_matrix(NY, CY).T)
    top = np.concatenate([high, low], 1)
    bottom = np.concatenate([high, np.zeros_like(low)], 1)
    return np.concatenate([top, bottom], 0)


MATRIX_X = compact_matrix(CX, HALO)


def split(value):
    high = value.astype(jnp.bfloat16)
    return high, (value - high.astype(jnp.float32)).astype(jnp.bfloat16)


def compact_rows(segment):
    even = [segment[i] + segment[15 - i] for i in range(8)]
    odd = [segment[i] - segment[15 - i] for i in range(8)]
    result = [None] * 8
    for i in range(4):
        both = sum(float(0.5 * (MATRIX_X[i, j] - MATRIX_X[i, 15 - j])) * odd[j] for j in range(8))
        diff = sum(float(0.5 * (MATRIX_X[i, j] + MATRIX_X[i, 15 - j])) * even[j] for j in range(8))
        result[i] = both + diff
        result[7 - i] = both - diff
    return result


def exchange_halves(top, bottom, low_lanes):
    moved = pltpu.roll(jnp.where(low_lanes, bottom, top), NY // 2, axis=1)
    return jnp.where(low_lanes, top, moved), jnp.where(low_lanes, moved, bottom)


def viscosity(temperature):
    return shear_resistance_reference * jnp.exp(sutherland_power_law * jnp.log(temperature))


def kernel(
    rho_hbm, mom_hbm, en_hbm, dh_hbm, dl_hbm, yc_hbm, out_ref,
    con, dh, dl, yc, prim, halo_lo, halo_hi, flux_lo, flux_hi,
    a1_send, a1_recv, a2_send, a2_recv, b1_send, b1_recv, b2_send, b2_recv,
    grad_x, grad_y, flux_x, pitch_in, span_x, rhs_h, rhs_l, dz_t,
    load_sem, a2a_send_sem, a2a_recv_sem, halo_send_sem, halo_recv_sem,
):
    gx = lax.axis_index("gx")
    me = lax.axis_index("gy")
    n_gx = lax.axis_size("gx")
    right, left = lax.rem(gx + 1, n_gx), lax.rem(gx + n_gx - 1, n_gx)

    loads = [
        pltpu.make_async_copy(rho_hbm, con.at[0], load_sem.at[0]),
        pltpu.make_async_copy(mom_hbm, con.at[pl.ds(1, 3)], load_sem.at[1]),
        pltpu.make_async_copy(en_hbm, con.at[4], load_sem.at[2]),
        pltpu.make_async_copy(yc_hbm, yc, load_sem.at[3]),
        pltpu.make_async_copy(dh_hbm, dh, load_sem.at[4]),
        pltpu.make_async_copy(dl_hbm, dl, load_sem.at[5]),
    ]
    for copy in loads:
        copy.start()

    barrier = pltpu.get_barrier_semaphore()

    def greet(k, carry):
        pl.semaphore_signal(
            barrier, inc=1, device_id={"gy": lax.rem(me + k, GY)}, device_id_type=MESH
        )
        return carry

    lax.fori_loop(1, GY, greet, 0)
    for neighbour in (left, right):
        pl.semaphore_signal(barrier, inc=1, device_id={"gx": neighbour}, device_id_type=MESH)

    low_lanes = lax.broadcasted_iota(jnp.int32, (HZ, NY), 1) < NY // 2

    def a2a(phase, send, recv, k):
        return pltpu.make_async_remote_copy(
            src_ref=send.at[lax.rem(me + k, GY)],
            dst_ref=recv.at[me],
            send_sem=a2a_send_sem.at[phase, k],
            recv_sem=a2a_recv_sem.at[phase, k],
            device_id={"gy": lax.rem(me + k, GY)},
            device_id_type=MESH,
        )

    def a2a_start(phase, send, recv):
        def body(k, carry):
            a2a(phase, send, recv, k).start()
            return carry

        lax.fori_loop(1, GY, body, 0)
        recv[me] = send[me]

    def a2a_wait_recv(phase, send, recv):
        def body(k, carry):
            a2a(phase, send, recv, k).wait_recv()
            return carry

        lax.fori_loop(1, GY, body, 0)

    def a2a_wait_send(phase, send, recv):
        def body(k, carry):
            a2a(phase, send, recv, k).wait_send()
            return carry

        lax.fori_loop(1, GY, body, 0)

    def halo_pair(source, lo, hi, slot):
        up = pltpu.make_async_remote_copy(
            src_ref=source.at[pl.ds(CX - HALO, HALO)], dst_ref=lo,
            send_sem=halo_send_sem.at[0, slot], recv_sem=halo_recv_sem.at[0, slot],
            device_id={"gx": right}, device_id_type=MESH,
        )
        down = pltpu.make_async_remote_copy(
            src_ref=source.at[pl.ds(0, HALO)], dst_ref=hi,
            send_sem=halo_send_sem.at[1, slot], recv_sem=halo_recv_sem.at[1, slot],
            device_id={"gx": left}, device_id_type=MESH,
        )
        return up, down

    for copy in loads[:3]:
        copy.wait()

    def first(x, carry):
        values = [con[f, x] for f in range(5)]
        for f in range(5):
            p0, p1 = exchange_halves(values[f][:HZ], values[f][HZ:], low_lanes)
            a1_send[2 * x, f] = p0
            a1_send[2 * x + 1, f] = p1
        inverse = 1.0 / values[0]
        speeds = [values[1 + i] * inverse for i in range(3)]
        kinetic = 0.5 * (
            values[1] * speeds[0] + values[2] * speeds[1] + values[3] * speeds[2]
        )
        temperature = (heat_ratio - 1.0) * (values[4] - kinetic) * inverse
        for f, value in enumerate(speeds + [temperature]):
            prim[f, x] = value
            high, low = split(value)
            rows = pl.ds(pl.multiple_of(x * ZB, ZB), ZB)
            pitch_in[f, rows, :NY] = high
            pitch_in[f, rows, NY:] = low
        return carry

    lax.fori_loop(0, CX, first, 0)

    pl.semaphore_wait(barrier, GY + 1)

    sources = [prim.at[0], prim.at[1], prim.at[2], prim.at[3], con.at[1]]
    halos = [halo_pair(sources[f], halo_lo.at[f], halo_hi.at[f], f) for f in range(5)]
    for f in (2, 0, 1, 3, 4):
        for copy in halos[f]:
            copy.start()
    a2a_start(0, a1_send, a1_recv)

    loads[3].wait()

    def pitch_derivative(f):
        product = jnp.dot(pitch_in[f], yc[...], preferred_element_type=jnp.float32)
        return (product[:, :NY] + product[:, NY:]).reshape(CX, ZB, NY)

    for f in range(4):
        grad_y[f] = pitch_derivative(f)

    def stream_derivative(own, lo, hi, emit):
        def body(t, carry):
            rows = pl.ds(pl.multiple_of(t * 8, 8), 8)
            segment = [lo[i, rows] for i in range(HALO)]
            segment += [own[i, rows] for i in range(CX)]
            segment += [hi[i, rows] for i in range(HALO)]
            for i, value in enumerate(compact_rows(segment)):
                emit(i, rows, value)
            return carry

        lax.fori_loop(0, ZB // 8, body, 0)

    def halo_wait(copies):
        for copy in copies:
            copy.wait_recv()

    def prim_x(f):
        halo_wait(halos[f])

        def emit(i, rows, value):
            grad_x[f, i, rows] = value

        stream_derivative(sources[f], halo_lo.at[f], halo_hi.at[f], emit)

    prim_x(2)
    prim_x(0)

    def extras(x, carry):
        values = [grad_x[2, x], grad_y[2, x], grad_x[0, x] + grad_y[1, x]]
        for f in range(3):
            p0, p1 = exchange_halves(values[f][:HZ], values[f][HZ:], low_lanes)
            a2_send[2 * x, f] = p0
            a2_send[2 * x + 1, f] = p1
        return carry

    lax.fori_loop(0, CX, extras, 0)
    a2a_start(1, a2_send, a2_recv)
    prim_x(1)
    prim_x(3)

    for copy in loads[4:]:
        copy.wait()
    a2a_wait_recv(0, a1_send, a1_recv)

    def span_first(s, carry):
        density, m1, m2, m3, energy = [a1_recv[s, f] for f in range(5)]
        inverse = 1.0 / density
        v1, v2, v3 = m1 * inverse, m2 * inverse, m3 * inverse
        kinetic = 0.5 * (m1 * v1 + m2 * v2 + m3 * v3)
        span_x[4, s] = (heat_ratio - 1.0) * (energy - kinetic) * inverse
        span_x[0, s] = v1
        span_x[1, s] = v2
        span_x[2, s] = v3
        span_x[3, s] = m3
        return carry

    lax.fori_loop(0, GY, span_first, 0, unroll=2)

    def build(fields):
        def body(s, carry):
            after = lax.rem(s + 1, GY)
            near_rows = pl.ds(pl.multiple_of(s * HZ, HZ), HZ)
            far_rows = pl.ds(pl.multiple_of(NZ // 2 + s * HZ, HZ), HZ)
            for f in fields:
                columns = pl.ds(f * NY, NY)
                here = span_x[f, s]
                other = pltpu.roll(
                    jnp.where(low_lanes, span_x[f, after], here), NY // 2, axis=1
                )
                high, low = split(here)
                rhs_h[near_rows, columns] = high
                rhs_l[near_rows, columns] = low
                high, low = split(other)
                rhs_h[far_rows, columns] = high
                rhs_l[far_rows, columns] = low
            return carry

        lax.fori_loop(0, GY, body, 0, unroll=2)

    def span_product(start, count):
        columns = pl.ds(start * NY, count * NY)
        high = rhs_h[:, columns]
        product = jnp.dot(dh[...], high, preferred_element_type=jnp.float32)
        product += jnp.dot(dh[...], rhs_l[:, columns], preferred_element_type=jnp.float32)
        product += jnp.dot(dl[...], high, preferred_element_type=jnp.float32)
        return product

    build(range(4))
    for pair in (0, 2):
        product = span_product(pair, 2)
        for f in range(2):
            b1_send[:, pair + f] = product[:, f * NY : (f + 1) * NY].reshape(GY, HZ, NY)
    a2a_start(2, b1_send, b1_recv)
    build([4])
    dz_t[...] = span_product(4, 1).reshape(GY, HZ, NY)

    a2a_wait_recv(1, a2_send, a2_recv)

    def span_second(s, carry):
        m1, m2, m3, energy = [a1_recv[s, f] for f in range(1, 5)]
        v1, v2, v3, temperature = [span_x[f, s] for f in (0, 1, 2, 4)]
        pressure = temperature * a1_recv[s, 0]
        dz1, dz2, dz3 = [b1_send[s, f] for f in range(3)]
        dx3, dy3, plane = [a2_recv[s, f] for f in range(3)]
        visc = viscosity(temperature)
        s13 = visc * (dz1 + dx3)
        s23 = visc * (dz2 + dy3)
        s33 = visc * (2.0 * dz3 - (2.0 / 3.0) * (plane + dz3))
        work = s13 * v1 + s23 * v2 + s33 * v3
        span_x[5, s] = m1 * v3 - s13
        span_x[6, s] = m2 * v3 - s23
        span_x[7, s] = m3 * v3 - s33 + pressure
        span_x[8, s] = (energy + pressure) * v3 - work - (visc * conduction) * dz_t[s]
        return carry

    lax.fori_loop(0, GY, span_second, 0, unroll=2)
    build(range(5, 9))
    for pair in (0, 2):
        product = span_product(5 + pair, 2)
        for f in range(2):
            b2_send[:, pair + f] = product[:, f * NY : (f + 1) * NY].reshape(GY, HZ, NY)
    a2a_start(3, b2_send, b2_recv)

    a2a_wait_recv(2, b1_send, b1_recv)

    def fluxes(x, carry):
        dz = []
        for f in range(4):
            top, bottom = exchange_halves(b1_recv[2 * x, f], b1_recv[2 * x + 1, f], low_lanes)
            dz.append(jnp.concatenate([top, bottom], 0))
        out_ref[0, x] = dz[3]
        density, m1, m2, m3, energy = [con[f, x] for f in range(5)]
        v1, v2, v3, temperature = [prim[f, x] for f in range(4)]
        pressure = temperature * density
        dx1, dx2, dx3, dxt = [grad_x[f, x] for f in range(4)]
        dy1, dy2, dy3, dyt = [grad_y[f, x] for f in range(4)]
        dz1, dz2, dz3 = dz[:3]
        visc = viscosity(temperature)
        heat = visc * conduction
        bulk = (2.0 / 3.0) * (dx1 + dy2 + dz3)
        total = energy + pressure
        s11 = visc * (2.0 * dx1 - bulk)
        s22 = visc * (2.0 * dy2 - bulk)
        s12 = visc * (dx2 + dy1)
        s13 = visc * (dx3 + dz1)
        s23 = visc * (dy3 + dz2)
        flux_x[0, x] = m1 * v1 + pressure - s11
        flux_x[1, x] = m2 * v1 - s12
        flux_x[2, x] = m3 * v1 - s13
        flux_x[3, x] = total * v1 - (s11 * v1 + s12 * v2 + s13 * v3) - heat * dxt
        pitch = [
            m2,
            m1 * v2 - s12,
            m2 * v2 + pressure - s22,
            m3 * v2 - s23,
            total * v2 - (s12 * v1 + s22 * v2 + s23 * v3) - heat * dyt,
        ]
        rows = pl.ds(pl.multiple_of(x * ZB, ZB), ZB)
        for f in range(5):
            high, low = split(pitch[f])
            pitch_in[f, rows, :NY] = high
            pitch_in[f, rows, NY:] = low
        return carry

    lax.fori_loop(0, CX, fluxes, 0)

    flux_halos = [
        halo_pair(flux_x.at[f], flux_lo.at[f], flux_hi.at[f], 5 + f) for f in range(4)
    ]
    for copies in flux_halos:
        for copy in copies:
            copy.start()

    out_ref[0] += pitch_derivative(0)
    for f in range(1, 5):
        out_ref[f] = pitch_derivative(f)

    def accumulate(f, own, lo, hi):
        def emit(i, rows, value):
            out_ref[f, i, rows] += value

        stream_derivative(own, lo, hi, emit)

    halo_wait(halos[4])
    accumulate(0, con.at[1], halo_lo.at[4], halo_hi.at[4])
    for f in range(4):
        halo_wait(flux_halos[f])
        accumulate(1 + f, flux_x.at[f], flux_lo.at[f], flux_hi.at[f])

    a2a_wait_recv(3, b2_send, b2_recv)

    def last(x, carry):
        for f in range(4):
            top, bottom = exchange_halves(b2_recv[2 * x, f], b2_recv[2 * x + 1, f], low_lanes)
            out_ref[1 + f, x] += jnp.concatenate([top, bottom], 0)
        return carry

    lax.fori_loop(0, CX, last, 0)

    a2a_wait_send(0, a1_send, a1_recv)
    a2a_wait_send(1, a2_send, a2_recv)
    a2a_wait_send(2, b1_send, b1_recv)
    a2a_wait_send(3, b2_send, b2_recv)
    for copies in halos + flux_halos:
        for copy in copies:
            copy.wait_send()


def per_device(mass_per_volume, momentum, energy):
    dh, dl = span_operand()
    yc = pitch_operand()
    f32, bf16 = jnp.float32, jnp.bfloat16
    field = (CX, ZB, NY)
    piece = (HZ, NY)
    spread = pl.pallas_call(
        kernel,
        out_shape=jax.ShapeDtypeStruct((5,) + field, f32),
        in_specs=[pl.BlockSpec(memory_space=pl.ANY)] * 6,
        out_specs=pl.BlockSpec(memory_space=pltpu.VMEM),
        scratch_shapes=[
            pltpu.VMEM((5,) + field, f32),
            pltpu.VMEM((NZ // 2, NZ), bf16),
            pltpu.VMEM((NZ // 2, NZ), bf16),
            pltpu.VMEM((2 * NY, 2 * NY), bf16),
            pltpu.VMEM((4,) + field, f32),
            pltpu.VMEM((5, HALO, ZB, NY), f32),
            pltpu.VMEM((5, HALO, ZB, NY), f32),
            pltpu.VMEM((4, HALO, ZB, NY), f32),
            pltpu.VMEM((4, HALO, ZB, NY), f32),
            pltpu.VMEM((GY, 5) + piece, f32),
            pltpu.VMEM((GY, 5) + piece, f32),
            pltpu.VMEM((GY, 3) + piece, f32),
            pltpu.VMEM((GY, 3) + piece, f32),
            pltpu.VMEM((GY, 4) + piece, f32),
            pltpu.VMEM((GY, 4) + piece, f32),
            pltpu.VMEM((GY, 4) + piece, f32),
            pltpu.VMEM((GY, 4) + piece, f32),
            pltpu.VMEM((4,) + field, f32),
            pltpu.VMEM((4,) + field, f32),
            pltpu.VMEM((4,) + field, f32),
            pltpu.VMEM((5, CX * ZB, 2 * NY), bf16),
            pltpu.VMEM((9, GY) + piece, f32),
            pltpu.VMEM((NZ, 9 * NY), bf16),
            pltpu.VMEM((NZ, 9 * NY), bf16),
            pltpu.VMEM((GY,) + piece, f32),
            pltpu.SemaphoreType.DMA((6,)),
            pltpu.SemaphoreType.DMA((4, GY)),
            pltpu.SemaphoreType.DMA((4, GY)),
            pltpu.SemaphoreType.DMA((2, 9)),
            pltpu.SemaphoreType.DMA((2, 9)),
        ],
        compiler_params=pltpu.CompilerParams(collective_id=0, has_side_effects=True),
    )(mass_per_volume, momentum, energy, jnp.asarray(dh), jnp.asarray(dl), jnp.asarray(yc))
    conserved = jnp.concatenate([mass_per_volume[None], momentum, energy[None]], 0)
    tendency = -spread
    return tendency, conserved + section_step * tendency


def solution(mesh):
    in_specs = (P("gx", "gy", None), P(None, "gx", "gy", None), P("gx", "gy", None))
    out_specs = (P(None, "gx", "gy", None), P(None, "gx", "gy", None))
    return jax.shard_map(
        per_device, mesh=mesh, in_specs=in_specs, out_specs=out_specs, check_vma=False
    )
```

```python
import jax
import jax.numpy as jnp
import ml_dtypes
import numpy as np
from jax import lax
from jax.experimental import pallas as pl
from jax.experimental.pallas import tpu as pltpu
from jax.sharding import PartitionSpec as P

CX = 8
CY = 8
NZ = 512
NY = 128
HALO = 4
GY = 16
ZB = NZ // GY
HZ = ZB // 2
MESH = pl.DeviceIdType.MESH

heat_ratio = 1.4
shear_resistance_reference = 0.08
sutherland_power_law = 0.7
prandtl = 0.72
section_step = 0.05
compact_alpha = 1.0 / 3.0
compact_near = 14.0 / 9.0
compact_far = 1.0 / 9.0
conduction = heat_ratio / ((heat_ratio - 1.0) * prandtl)


def tridiagonal_inverse_product(length, stencil):
    solved = np.array(stencil)
    upper_ratio = np.zeros(length)
    for row_index in range(length):
        if row_index == 0:
            pivot_value = 1.0
            solved[row_index] = solved[row_index] / pivot_value
        else:
            pivot_value = 1.0 - compact_alpha * upper_ratio[row_index - 1]
            solved[row_index] = (
                solved[row_index] - compact_alpha * solved[row_index - 1]
            ) / pivot_value
        upper_ratio[row_index] = compact_alpha / pivot_value
    for row_index in range(length - 2, -1, -1):
        solved[row_index] = solved[row_index] - upper_ratio[row_index] * solved[row_index + 1]
    return solved


def compact_matrix(block_size, margin):
    length = block_size + 2 * margin
    stencil = compact_near / 2.0 * (np.eye(length, k=1) - np.eye(length, k=-1))
    stencil = stencil + compact_far / 4.0 * (np.eye(length, k=2) - np.eye(length, k=-2))
    inverse_product = tridiagonal_inverse_product(length, stencil)
    return inverse_product[margin : margin + block_size]


def pitch_matrix(total, block_size):
    matrix = compact_matrix(block_size, HALO)
    result = np.zeros((total, total))
    rows_all = np.arange(total)
    block_start = rows_all // block_size * block_size
    for offset in range(block_size + 2 * HALO):
        columns = (block_start - HALO + offset) % total
        result[rows_all, columns] += matrix[rows_all % block_size, offset]
    return result


def span_kernel(offsets, total):
    angles = np.pi * offsets / total
    signs = np.where(offsets % 2 == 0, 1.0, -1.0)
    zero = offsets % total == 0
    sines = np.where(zero, 1.0, np.sin(angles))
    return np.where(zero, 0.0, np.pi / total * signs * np.cos(angles) / sines)


def high_low(matrix):
    high = matrix.astype(ml_dtypes.bfloat16)
    low = (matrix - high.astype(np.float64)).astype(ml_dtypes.bfloat16)
    return high, low


def span_operand():
    z = (np.arange(GY)[:, None] * ZB + np.arange(HZ)[None, :]).reshape(-1)
    near = span_kernel(z[:, None] - z[None, :], NZ)
    far = span_kernel(z[:, None] - (z[None, :] + HZ), NZ)
    return high_low(np.concatenate([near, far], 1))


def pitch_operand():
    high, low = high_low(pitch_matrix(NY, CY).T)
    top = np.concatenate([high, low], 1)
    bottom = np.concatenate([high, np.zeros_like(low)], 1)
    return np.concatenate([top, bottom], 0)


MATRIX_X = compact_matrix(CX, HALO)


def split(value):
    high = value.astype(jnp.bfloat16)
    return high, (value - high.astype(jnp.float32)).astype(jnp.bfloat16)


def compact_rows(segment):
    even = [segment[i] + segment[15 - i] for i in range(8)]
    odd = [segment[i] - segment[15 - i] for i in range(8)]
    result = [None] * 8
    for i in range(4):
        both = sum(float(0.5 * (MATRIX_X[i, j] - MATRIX_X[i, 15 - j])) * odd[j] for j in range(8))
        diff = sum(float(0.5 * (MATRIX_X[i, j] + MATRIX_X[i, 15 - j])) * even[j] for j in range(8))
        result[i] = both + diff
        result[7 - i] = both - diff
    return result


def exchange_halves(top, bottom, low_lanes):
    moved = pltpu.roll(jnp.where(low_lanes, bottom, top), NY // 2, axis=1)
    return jnp.where(low_lanes, top, moved), jnp.where(low_lanes, moved, bottom)


def viscosity(temperature):
    return shear_resistance_reference * jnp.exp(sutherland_power_law * jnp.log(temperature))


STEPS = [
    (dx, dy, dc)
    for dc in range(2)
    for dx, dy in ((2, 1), (1, 1), (3, 1), (2, 0), (0, 1), (1, 0), (3, 0))
] + [(0, 0, 1)]


def kernel(
    rho_hbm, mom_hbm, en_hbm, dh_hbm, dl_hbm, yc_hbm, out_ref, con,
    dh, dl, yc, prim, halo_lo, halo_hi, flux_lo, flux_hi,
    speed_send, speed_recv, state_send, state_recv, cross_send, cross_recv,
    slope_send, slope_recv, slope2_send, slope2_recv, div_send, div_recv,
    grad_x, grad_y, flux_x, keep, pitch_in, span_x, rhs_h, rhs_l, dz_t, span_visc,
    load_sem, a2a_send_sem, a2a_recv_sem, halo_send_sem, halo_recv_sem,
):
    gx = lax.axis_index("gx")
    me = lax.axis_index("gy")
    n_gx = lax.axis_size("gx")
    right, left = lax.rem(gx + 1, n_gx), lax.rem(gx + n_gx - 1, n_gx)
    chip_x, chip_y, core = me // 4, lax.rem(me // 2, 2), lax.rem(me, 2)
    partners = [
        lax.rem(chip_x + dx, 4) * 4 + lax.rem(chip_y + dy, 2) * 2 + lax.rem(core + dc, 2)
        for dx, dy, dc in STEPS
    ]

    loads = [
        pltpu.make_async_copy(rho_hbm, con.at[0], load_sem.at[0]),
        pltpu.make_async_copy(mom_hbm, con.at[pl.ds(1, 3)], load_sem.at[1]),
        pltpu.make_async_copy(en_hbm, con.at[4], load_sem.at[2]),
        pltpu.make_async_copy(yc_hbm, yc, load_sem.at[3]),
        pltpu.make_async_copy(dh_hbm, dh, load_sem.at[4]),
        pltpu.make_async_copy(dl_hbm, dl, load_sem.at[5]),
    ]
    for copy in loads:
        copy.start()

    barrier = pltpu.get_barrier_semaphore()
    for partner in partners:
        pl.semaphore_signal(barrier, inc=1, device_id={"gy": partner}, device_id_type=MESH)
    for neighbour in (left, right):
        pl.semaphore_signal(barrier, inc=1, device_id={"gx": neighbour}, device_id_type=MESH)

    low_lanes = lax.broadcasted_iota(jnp.int32, (HZ, NY), 1) < NY // 2

    def a2a(phase, send, recv, step, partner):
        return pltpu.make_async_remote_copy(
            src_ref=send.at[partner],
            dst_ref=recv.at[me],
            send_sem=a2a_send_sem.at[phase, step],
            recv_sem=a2a_recv_sem.at[phase, step],
            device_id={"gy": partner},
            device_id_type=MESH,
        )

    def a2a_start(phase, send, recv):
        for step, partner in enumerate(partners):
            a2a(phase, send, recv, step, partner).start()
        recv[me] = send[me]

    def a2a_wait_recv(phase, send, recv):
        def body(step, carry):
            a2a(phase, send, recv, step, partners[0]).wait_recv()
            return carry

        lax.fori_loop(0, GY - 1, body, 0)

    def a2a_wait_send(phase, send, recv):
        def body(step, carry):
            a2a(phase, send, recv, step, partners[0]).wait_send()
            return carry

        lax.fori_loop(0, GY - 1, body, 0)

    def halo_pair(source, lo, hi, slot):
        up = pltpu.make_async_remote_copy(
            src_ref=source.at[pl.ds(CX - HALO, HALO)], dst_ref=lo,
            send_sem=halo_send_sem.at[0, slot], recv_sem=halo_recv_sem.at[0, slot],
            device_id={"gx": right}, device_id_type=MESH,
        )
        down = pltpu.make_async_remote_copy(
            src_ref=source.at[pl.ds(0, HALO)], dst_ref=hi,
            send_sem=halo_send_sem.at[1, slot], recv_sem=halo_recv_sem.at[1, slot],
            device_id={"gx": left}, device_id_type=MESH,
        )
        return up, down

    def pack(send, slot, x, value):
        p0, p1 = exchange_halves(value[:HZ], value[HZ:], low_lanes)
        send[2 * x, slot] = p0
        send[2 * x + 1, slot] = p1

    def unpack(recv, slot, x):
        top, bottom = exchange_halves(recv[2 * x, slot], recv[2 * x + 1, slot], low_lanes)
        return jnp.concatenate([top, bottom], 0)

    def pitch_store(f, x, value):
        high, low = split(value)
        rows = pl.ds(pl.multiple_of(x * ZB, ZB), ZB)
        pitch_in[f, rows, :NY] = high
        pitch_in[f, rows, NY:] = low

    for copy in loads[:3]:
        copy.wait()

    def first(x, carry):
        density, m1, m2, m3, energy = [con[f, x] for f in range(5)]
        inverse = 1.0 / density
        v1, v2, v3 = m1 * inverse, m2 * inverse, m3 * inverse
        kinetic = 0.5 * (m1 * v1 + m2 * v2 + m3 * v3)
        temperature = (heat_ratio - 1.0) * (energy - kinetic) * inverse
        pack(speed_send, 0, x, v1)
        pack(speed_send, 1, x, v3)
        pack(state_send, 0, x, v2)
        pack(state_send, 1, x, density)
        pack(state_send, 2, x, temperature)
        for f, value in enumerate((v1, v2, v3, temperature)):
            prim[f, x] = value
            pitch_store(f, x, value)
        keep[0, x] = viscosity(temperature)
        return carry

    lax.fori_loop(0, CX, first, 0)

    pl.semaphore_wait(barrier, GY + 1)

    sources = [prim.at[0], prim.at[1], prim.at[2], prim.at[3], con.at[1]]
    halos = [halo_pair(sources[f], halo_lo.at[f], halo_hi.at[f], f) for f in range(5)]
    for f in (2, 0):
        for copy in halos[f]:
            copy.start()
    a2a_start(0, speed_send, speed_recv)
    a2a_start(1, state_send, state_recv)
    for f in (1, 3, 4):
        for copy in halos[f]:
            copy.start()

    loads[3].wait()

    def pitch_derivative(f):
        product = jnp.dot(pitch_in[f], yc[...], preferred_element_type=jnp.float32)
        return (product[:, :NY] + product[:, NY:]).reshape(CX, ZB, NY)

    for f in range(4):
        grad_y[f] = pitch_derivative(f)

    def stream_derivative(own, lo, hi, emit):
        def body(t, carry):
            rows = pl.ds(pl.multiple_of(t * 8, 8), 8)
            segment = [lo[i, rows] for i in range(HALO)]
            segment += [own[i, rows] for i in range(CX)]
            segment += [hi[i, rows] for i in range(HALO)]
            for i, value in enumerate(compact_rows(segment)):
                emit(i, rows, value)
            return carry

        lax.fori_loop(0, ZB // 8, body, 0)

    def halo_wait(copies):
        for copy in copies:
            copy.wait_recv()

    def prim_x(f):
        halo_wait(halos[f])

        def emit(i, rows, value):
            grad_x[f, i, rows] = value

        stream_derivative(sources[f], halo_lo.at[f], halo_hi.at[f], emit)

    prim_x(2)
    prim_x(0)

    def extras(x, carry):
        pack(cross_send, 0, x, grad_x[2, x])
        pack(cross_send, 1, x, grad_y[2, x])
        pack(cross_send, 2, x, grad_x[0, x] + grad_y[1, x])
        return carry

    lax.fori_loop(0, CX, extras, 0)
    a2a_start(2, cross_send, cross_recv)

    def build(fields):
        def body(s, carry):
            after = lax.rem(s + 1, GY)
            near_rows = pl.ds(pl.multiple_of(s * HZ, HZ), HZ)
            far_rows = pl.ds(pl.multiple_of(NZ // 2 + s * HZ, HZ), HZ)
            for column, fetch in fields:
                columns = pl.ds(column * NY, NY)
                here = fetch(s)
                other = pltpu.roll(jnp.where(low_lanes, fetch(after), here), NY // 2, axis=1)
                high, low = split(here)
                rhs_h[near_rows, columns] = high
                rhs_l[near_rows, columns] = low
                high, low = split(other)
                rhs_h[far_rows, columns] = high
                rhs_l[far_rows, columns] = low
            return carry

        lax.fori_loop(0, GY, body, 0, unroll=2)

    def span_product(start, count):
        columns = pl.ds(start * NY, count * NY)
        high = rhs_h[:, columns]
        product = jnp.dot(dh[...], high, preferred_element_type=jnp.float32)
        product += jnp.dot(dh[...], rhs_l[:, columns], preferred_element_type=jnp.float32)
        product += jnp.dot(dl[...], high, preferred_element_type=jnp.float32)
        return [
            product[:, f * NY : (f + 1) * NY].reshape(GY, HZ, NY) for f in range(count)
        ]

    for copy in loads[4:]:
        copy.wait()
    a2a_wait_recv(0, speed_send, speed_recv)
    build([(0, lambda s: speed_recv[s, 0]), (1, lambda s: speed_recv[s, 1])])
    for f, value in enumerate(span_product(0, 2)):
        slope_send[:, f] = value
    a2a_start(3, slope_send, slope_recv)

    a2a_wait_recv(1, state_send, state_recv)

    def span_first(s, carry):
        span_x[0, s] = state_recv[s, 1] * speed_recv[s, 1]
        span_visc[s] = viscosity(state_recv[s, 2])
        return carry

    lax.fori_loop(0, GY, span_first, 0, unroll=2)
    build([(2, lambda s: state_recv[s, 0]), (3, lambda s: span_x[0, s])])
    for f, value in enumerate(span_product(2, 2)):
        slope2_send[:, f] = value
    a2a_start(4, slope2_send, slope2_recv)
    build([(4, lambda s: state_recv[s, 2])])
    dz_t[...] = span_product(4, 1)[0]

    prim_x(1)
    prim_x(3)

    a2a_wait_recv(2, cross_send, cross_recv)

    def span_second(s, carry):
        v1, v3 = speed_recv[s, 0], speed_recv[s, 1]
        v2, density, temperature = [state_recv[s, f] for f in range(3)]
        m3 = span_x[0, s]
        pressure = temperature * density
        enthalpy = (heat_ratio / (heat_ratio - 1.0)) * pressure + 0.5 * density * (
            v1 * v1 + v2 * v2 + v3 * v3
        )
        dz1, dz3, dz2 = slope_send[s, 0], slope_send[s, 1], slope2_send[s, 0]
        dx3, dy3, plane = [cross_recv[s, f] for f in range(3)]
        visc = span_visc[s]
        s13 = visc * (dz1 + dx3)
        s23 = visc * (dz2 + dy3)
        s33 = visc * (2.0 * dz3 - (2.0 / 3.0) * (plane + dz3))
        work = s13 * v1 + s23 * v2 + s33 * v3
        span_x[1, s] = m3 * v1 - s13
        span_x[2, s] = m3 * v2 - s23
        span_x[3, s] = m3 * v3 - s33 + pressure
        span_x[4, s] = enthalpy * v3 - work - (visc * conduction) * dz_t[s]
        return carry

    lax.fori_loop(0, GY, span_second, 0, unroll=2)
    build([(5 + f, lambda s, f=f: span_x[1 + f, s]) for f in range(4)])
    for pair in (0, 2):
        for f, value in enumerate(span_product(5 + pair, 2)):
            div_send[:, pair + f] = value
    a2a_start(5, div_send, div_recv)

    a2a_wait_recv(3, slope_send, slope_recv)

    def stream_flux(x, carry):
        dz1, dz3 = unpack(slope_recv, 0, x), unpack(slope_recv, 1, x)
        density, m1, m2, m3, energy = [con[f, x] for f in range(5)]
        v1, v2, v3, temperature = [prim[f, x] for f in range(4)]
        pressure = temperature * density
        dx1, dx2, dx3, dxt = [grad_x[f, x] for f in range(4)]
        visc = keep[0, x]
        bulk = (2.0 / 3.0) * (dx1 + grad_y[1, x] + dz3)
        s11 = visc * (2.0 * dx1 - bulk)
        s12 = visc * (dx2 + grad_y[0, x])
        s13 = visc * (dx3 + dz1)
        flux_x[0, x] = m1 * v1 + pressure - s11
        flux_x[1, x] = m2 * v1 - s12
        flux_x[2, x] = m3 * v1 - s13
        work = s11 * v1 + s12 * v2 + s13 * v3
        flux_x[3, x] = (energy + pressure) * v1 - work - (visc * conduction) * dxt
        keep[1, x] = bulk
        keep[2, x] = s12
        return carry

    lax.fori_loop(0, CX, stream_flux, 0)
    flux_halos = [
        halo_pair(flux_x.at[f], flux_lo.at[f], flux_hi.at[f], 5 + f) for f in range(4)
    ]
    for copies in flux_halos:
        for copy in copies:
            copy.start()

    a2a_wait_recv(4, slope2_send, slope2_recv)

    def pitch_flux(x, carry):
        dz2 = unpack(slope2_recv, 0, x)
        out_ref[0, x] = unpack(slope2_recv, 1, x)
        density, m1, m2, m3, energy = [con[f, x] for f in range(5)]
        v1, v2, v3, temperature = [prim[f, x] for f in range(4)]
        pressure = temperature * density
        visc, bulk, s12 = [keep[f, x] for f in range(3)]
        s22 = visc * (2.0 * grad_y[1, x] - bulk)
        s23 = visc * (grad_y[2, x] + dz2)
        work = s12 * v1 + s22 * v2 + s23 * v3
        pitch_store(0, x, m2)
        pitch_store(1, x, m1 * v2 - s12)
        pitch_store(2, x, m2 * v2 + pressure - s22)
        pitch_store(3, x, m3 * v2 - s23)
        flux = (energy + pressure) * v2 - work - (visc * conduction) * grad_y[3, x]
        pitch_store(4, x, flux)
        return carry

    lax.fori_loop(0, CX, pitch_flux, 0)
    out_ref[0] += pitch_derivative(0)
    for f in range(1, 5):
        out_ref[f] = pitch_derivative(f)

    def accumulate(f, own, lo, hi):
        def emit(i, rows, value):
            out_ref[f, i, rows] += value

        stream_derivative(own, lo, hi, emit)

    halo_wait(halos[4])
    accumulate(0, con.at[1], halo_lo.at[4], halo_hi.at[4])
    for f in range(4):
        halo_wait(flux_halos[f])
        accumulate(1 + f, flux_x.at[f], flux_lo.at[f], flux_hi.at[f])

    a2a_wait_recv(5, div_send, div_recv)

    def last(x, carry):
        for f in range(4):
            out_ref[1 + f, x] += unpack(div_recv, f, x)
        return carry

    lax.fori_loop(0, CX, last, 0)

    a2a_wait_send(0, speed_send, speed_recv)
    a2a_wait_send(1, state_send, state_recv)
    a2a_wait_send(2, cross_send, cross_recv)
    a2a_wait_send(3, slope_send, slope_recv)
    a2a_wait_send(4, slope2_send, slope2_recv)
    a2a_wait_send(5, div_send, div_recv)
    for copies in halos + flux_halos:
        for copy in copies:
            copy.wait_send()


def per_device(mass_per_volume, momentum, energy):
    dh, dl = span_operand()
    yc = pitch_operand()
    f32, bf16 = jnp.float32, jnp.bfloat16
    field = (CX, ZB, NY)
    piece = (HZ, NY)
    spread, conserved = pl.pallas_call(
        kernel,
        out_shape=[jax.ShapeDtypeStruct((5,) + field, f32)] * 2,
        in_specs=[pl.BlockSpec(memory_space=pltpu.HBM)] * 6,
        out_specs=[pl.BlockSpec(memory_space=pltpu.VMEM)] * 2,
        scratch_shapes=[
            pltpu.VMEM((NZ // 2, NZ), bf16),
            pltpu.VMEM((NZ // 2, NZ), bf16),
            pltpu.VMEM((2 * NY, 2 * NY), bf16),
            pltpu.VMEM((4,) + field, f32),
            pltpu.VMEM((5, HALO, ZB, NY), f32),
            pltpu.VMEM((5, HALO, ZB, NY), f32),
            pltpu.VMEM((4, HALO, ZB, NY), f32),
            pltpu.VMEM((4, HALO, ZB, NY), f32),
        ]
        + [pltpu.VMEM((GY, n) + piece, f32) for n in (2, 3, 3, 2, 2, 4) for _ in range(2)]
        + [
            pltpu.VMEM((4,) + field, f32),
            pltpu.VMEM((4,) + field, f32),
            pltpu.VMEM((4,) + field, f32),
            pltpu.VMEM((3,) + field, f32),
            pltpu.VMEM((5, CX * ZB, 2 * NY), bf16),
            pltpu.VMEM((5, GY) + piece, f32),
            pltpu.VMEM((NZ, 9 * NY), bf16),
            pltpu.VMEM((NZ, 9 * NY), bf16),
            pltpu.VMEM((GY,) + piece, f32),
            pltpu.VMEM((GY,) + piece, f32),
            pltpu.SemaphoreType.DMA((6,)),
            pltpu.SemaphoreType.DMA((6, GY - 1)),
            pltpu.SemaphoreType.DMA((6, GY - 1)),
            pltpu.SemaphoreType.DMA((2, 9)),
            pltpu.SemaphoreType.DMA((2, 9)),
        ],
        compiler_params=pltpu.CompilerParams(
            collective_id=0, has_side_effects=True, vmem_limit_bytes=24 * 1024 * 1024
        ),
    )(*[pltpu.with_memory_space_constraint(x, pltpu.HBM) for x in (mass_per_volume, momentum, energy, jnp.asarray(dh), jnp.asarray(dl), jnp.asarray(yc))])
    tendency = -spread
    return tendency, conserved + section_step * tendency


def solution(mesh):
    in_specs = (P("gx", "gy", None), P(None, "gx", "gy", None), P("gx", "gy", None))
    out_specs = (P(None, "gx", "gy", None), P(None, "gx", "gy", None))
    return jax.shard_map(
        per_device, mesh=mesh, in_specs=in_specs, out_specs=out_specs, check_vma=False
    )
```

```python
import jax
import jax.numpy as jnp
import ml_dtypes
import numpy as np
from jax import lax
from jax.experimental import pallas as pl
from jax.experimental.pallas import tpu as pltpu
from jax.sharding import PartitionSpec as P

CX = 8
CY = 8
NZ = 512
NY = 128
HALO = 4
GY = 16
ZB = NZ // GY
HZ = ZB // 2
MESH = pl.DeviceIdType.MESH

heat_ratio = 1.4
shear_resistance_reference = 0.08
sutherland_power_law = 0.7
prandtl = 0.72
section_step = 0.05
compact_alpha = 1.0 / 3.0
compact_near = 14.0 / 9.0
compact_far = 1.0 / 9.0
conduction = heat_ratio / ((heat_ratio - 1.0) * prandtl)


def tridiagonal_inverse_product(length, stencil):
    solved = np.array(stencil)
    upper_ratio = np.zeros(length)
    for row_index in range(length):
        if row_index == 0:
            pivot_value = 1.0
            solved[row_index] = solved[row_index] / pivot_value
        else:
            pivot_value = 1.0 - compact_alpha * upper_ratio[row_index - 1]
            solved[row_index] = (
                solved[row_index] - compact_alpha * solved[row_index - 1]
            ) / pivot_value
        upper_ratio[row_index] = compact_alpha / pivot_value
    for row_index in range(length - 2, -1, -1):
        solved[row_index] = solved[row_index] - upper_ratio[row_index] * solved[row_index + 1]
    return solved


def compact_matrix(block_size, margin):
    length = block_size + 2 * margin
    stencil = compact_near / 2.0 * (np.eye(length, k=1) - np.eye(length, k=-1))
    stencil = stencil + compact_far / 4.0 * (np.eye(length, k=2) - np.eye(length, k=-2))
    inverse_product = tridiagonal_inverse_product(length, stencil)
    return inverse_product[margin : margin + block_size]


def pitch_matrix(total, block_size):
    matrix = compact_matrix(block_size, HALO)
    result = np.zeros((total, total))
    rows_all = np.arange(total)
    block_start = rows_all // block_size * block_size
    for offset in range(block_size + 2 * HALO):
        columns = (block_start - HALO + offset) % total
        result[rows_all, columns] += matrix[rows_all % block_size, offset]
    return result


def span_kernel(offsets, total):
    angles = np.pi * offsets / total
    signs = np.where(offsets % 2 == 0, 1.0, -1.0)
    zero = offsets % total == 0
    sines = np.where(zero, 1.0, np.sin(angles))
    return np.where(zero, 0.0, np.pi / total * signs * np.cos(angles) / sines)


def high_low(matrix):
    high = matrix.astype(ml_dtypes.bfloat16)
    low = (matrix - high.astype(np.float64)).astype(ml_dtypes.bfloat16)
    return high, low


def span_operand():
    z = (np.arange(GY)[:, None] * ZB + np.arange(HZ)[None, :]).reshape(-1)
    near = span_kernel(z[:, None] - z[None, :], NZ)
    far = span_kernel(z[:, None] - (z[None, :] + HZ), NZ)
    return high_low(np.concatenate([near, far], 1))


def pitch_operand():
    high, low = high_low(pitch_matrix(NY, CY).T)
    top = np.concatenate([high, low], 1)
    bottom = np.concatenate([high, np.zeros_like(low)], 1)
    return np.concatenate([top, bottom], 0)


def half_pitch_operand():
    matrix = pitch_matrix(NY, CY).T
    half = NY // 2
    near, far = matrix[:half, :half], matrix[half:, :half]
    assert np.allclose(near, matrix[half:, half:]) and np.allclose(far, matrix[:half, half:])
    stacked = np.concatenate([np.kron(np.eye(2), near), np.kron(np.eye(2), far)], 0)
    return np.concatenate(high_low(stacked), 1)


MATRIX_X = compact_matrix(CX, HALO)
EDGE = HALO - 1
OUTERMOST = float(MATRIX_X[0, 0] / MATRIX_X[0, 1])
assert np.allclose(MATRIX_X[:, 0], OUTERMOST * MATRIX_X[:, 1], rtol=1e-9, atol=1e-12)
SEGMENT = CX + 2 * EDGE
MATRIX_E = MATRIX_X[:, 1:-1]


def split(value):
    high = value.astype(jnp.bfloat16)
    return high, (value - high.astype(jnp.float32)).astype(jnp.bfloat16)


def compact_rows(segment):
    half, end = SEGMENT // 2, SEGMENT - 1
    even = [segment[i] + segment[end - i] for i in range(half)]
    odd = [segment[i] - segment[end - i] for i in range(half)]
    result = [None] * CX
    for i in range(CX // 2):
        row = MATRIX_E[i]
        both = sum(float(0.5 * (row[j] - row[end - j])) * odd[j] for j in range(half))
        diff = sum(float(0.5 * (row[j] + row[end - j])) * even[j] for j in range(half))
        result[i] = both + diff
        result[CX - 1 - i] = both - diff
    return result


def exchange_halves(top, bottom, low_lanes):
    moved = pltpu.roll(jnp.where(low_lanes, bottom, top), NY // 2, axis=1)
    return jnp.where(low_lanes, top, moved), jnp.where(low_lanes, moved, bottom)


def viscosity(temperature):
    return shear_resistance_reference * jnp.exp(sutherland_power_law * jnp.log(temperature))


STEPS = [
    (dx, dy, dc)
    for dc in range(2)
    for dx, dy in ((2, 1), (1, 1), (3, 1), (2, 0), (0, 1), (1, 0), (3, 0))
] + [(0, 0, 1)]


def kernel(
    rho_hbm, mom_hbm, en_hbm, dh_hbm, dl_hbm, yc_hbm, ys_hbm, out_ref, con,
    dh, dl, yc, ys, prim, edges, halo_lo, halo_hi, flux_lo, flux_hi,
    speed_send, speed_recv, state_send, state_recv, cross_send, cross_recv,
    slope_send, slope_recv, slope2_send, slope2_recv, div_send, div_recv,
    grad_x, grad_y, flux_x, keep, pitch_in, span_x, rhs_h, rhs_l, dz_t, span_visc,
    sib_value, sib_send_buf, span_in, span_dy, dz_v2, sib_send_sem, sib_recv_sem,
    load_sem, a2a_send_sem, a2a_recv_sem, halo_send_sem, halo_recv_sem,
):
    gx = lax.axis_index("gx")
    me = lax.axis_index("gy")
    n_gx = lax.axis_size("gx")
    right, left = lax.rem(gx + 1, n_gx), lax.rem(gx + n_gx - 1, n_gx)
    chip_x, chip_y, core = me // 4, lax.rem(me // 2, 2), lax.rem(me, 2)
    partners = [
        lax.rem(chip_x + dx, 4) * 4 + lax.rem(chip_y + dy, 2) * 2 + lax.rem(core + dc, 2)
        for dx, dy, dc in STEPS
    ]

    loads = [
        pltpu.make_async_copy(rho_hbm, con.at[0], load_sem.at[0]),
        pltpu.make_async_copy(mom_hbm, con.at[pl.ds(1, 3)], load_sem.at[1]),
        pltpu.make_async_copy(en_hbm, con.at[4], load_sem.at[2]),
        pltpu.make_async_copy(yc_hbm, yc, load_sem.at[3]),
        pltpu.make_async_copy(dh_hbm, dh, load_sem.at[4]),
        pltpu.make_async_copy(dl_hbm, dl, load_sem.at[5]),
        pltpu.make_async_copy(ys_hbm, ys, load_sem.at[6]),
    ]
    for copy in loads:
        copy.start()

    barrier = pltpu.get_barrier_semaphore()
    sibling = partners[-1]
    for partner in partners:
        pl.semaphore_signal(barrier, inc=1, device_id={"gy": partner}, device_id_type=MESH)
    for neighbour in (left, right):
        pl.semaphore_signal(barrier, inc=1, device_id={"gx": neighbour}, device_id_type=MESH)

    low_lanes = lax.broadcasted_iota(jnp.int32, (HZ, NY), 1) < NY // 2

    def a2a(phase, send, recv, step, partner):
        return pltpu.make_async_remote_copy(
            src_ref=send.at[partner],
            dst_ref=recv.at[me],
            send_sem=a2a_send_sem.at[phase, step],
            recv_sem=a2a_recv_sem.at[phase, step],
            device_id={"gy": partner},
            device_id_type=MESH,
        )

    def a2a_start(phase, send, recv):
        for step, partner in enumerate(partners):
            a2a(phase, send, recv, step, partner).start()
        recv[me] = send[me]

    def a2a_wait_recv(phase, send, recv):
        def body(step, carry):
            a2a(phase, send, recv, step, partners[0]).wait_recv()
            return carry

        lax.fori_loop(0, GY - 1, body, 0)

    def a2a_wait_send(phase, send, recv):
        def body(step, carry):
            a2a(phase, send, recv, step, partners[0]).wait_send()
            return carry

        lax.fori_loop(0, GY - 1, body, 0)

    def halo_pair(lo, hi, slot):
        up = pltpu.make_async_remote_copy(
            src_ref=edges.at[slot, 0], dst_ref=lo,
            send_sem=halo_send_sem.at[0, slot], recv_sem=halo_recv_sem.at[0, slot],
            device_id={"gx": right}, device_id_type=MESH,
        )
        down = pltpu.make_async_remote_copy(
            src_ref=edges.at[slot, 1], dst_ref=hi,
            send_sem=halo_send_sem.at[1, slot], recv_sem=halo_recv_sem.at[1, slot],
            device_id={"gx": left}, device_id_type=MESH,
        )
        return up, down

    def edge_store(source, slot):
        edges[slot, 0, 0] = source[CX - 3] + OUTERMOST * source[CX - 4]
        edges[slot, 0, 1] = source[CX - 2]
        edges[slot, 0, 2] = source[CX - 1]
        edges[slot, 1, 0] = source[0]
        edges[slot, 1, 1] = source[1]
        edges[slot, 1, 2] = source[2] + OUTERMOST * source[3]

    def sibling_copy(source, slot):
        return pltpu.make_async_remote_copy(
            src_ref=source, dst_ref=sib_value.at[slot],
            send_sem=sib_send_sem.at[slot], recv_sem=sib_recv_sem.at[slot],
            device_id={"gy": sibling}, device_id_type=MESH,
        )

    def pack(send, slot, x, value):
        p0, p1 = exchange_halves(value[:HZ], value[HZ:], low_lanes)
        send[2 * x, slot] = p0
        send[2 * x + 1, slot] = p1

    def unpack(recv, slot, x):
        top, bottom = exchange_halves(recv[2 * x, slot], recv[2 * x + 1, slot], low_lanes)
        return jnp.concatenate([top, bottom], 0)

    def pitch_store(f, x, value):
        high, low = split(value)
        rows = pl.ds(pl.multiple_of(x * ZB, ZB), ZB)
        pitch_in[f, rows, :NY] = high
        pitch_in[f, rows, NY:] = low

    for copy in loads[:3]:
        copy.wait()

    def first(x, carry):
        density, m1, m2, m3, energy = [con[f, x] for f in range(5)]
        inverse = 1.0 / density
        v1, v2, v3 = m1 * inverse, m2 * inverse, m3 * inverse
        kinetic = 0.5 * (m1 * v1 + m2 * v2 + m3 * v3)
        temperature = (heat_ratio - 1.0) * (energy - kinetic) * inverse
        pack(speed_send, 0, x, v1)
        pack(speed_send, 1, x, v3)
        pack(state_send, 0, x, v2)
        pack(state_send, 1, x, density)
        pack(state_send, 2, x, temperature)
        for f, value in enumerate((v1, v2, v3, temperature)):
            prim[f, x] = value
            pitch_store(f, x, value)
        keep[0, x] = viscosity(temperature)
        return carry

    lax.fori_loop(0, CX, first, 0)

    sources = [prim.at[0], prim.at[1], prim.at[2], prim.at[3], con.at[1]]
    for f in range(5):
        edge_store(sources[f], f)

    pl.semaphore_wait(barrier, GY + 1)
    a2a_start(0, speed_send, speed_recv)
    a2a_start(1, state_send, state_recv)

    halos = [halo_pair(halo_lo.at[f], halo_hi.at[f], f) for f in range(5)]
    for f in (2, 0, 1, 3, 4):
        for copy in halos[f]:
            copy.start()

    loads[3].wait()

    def pitch_derivative(f):
        product = jnp.dot(pitch_in[f], yc[...], preferred_element_type=jnp.float32)
        return (product[:, :NY] + product[:, NY:]).reshape(CX, ZB, NY)

    for f in (0, 1, 3):
        grad_y[f] = pitch_derivative(f)

    def stream_derivative(own, lo, hi, emit):
        def body(t, carry):
            rows = pl.ds(pl.multiple_of(t * 8, 8), 8)
            segment = [lo[i, rows] for i in range(EDGE)]
            segment += [own[i, rows] for i in range(CX)]
            segment += [hi[i, rows] for i in range(EDGE)]
            for i, value in enumerate(compact_rows(segment)):
                emit(i, rows, value)
            return carry

        lax.fori_loop(0, ZB // 8, body, 0)

    def halo_wait(copies):
        for copy in copies:
            copy.wait_recv()

    def prim_x(f):
        halo_wait(halos[f])

        def emit(i, rows, value):
            grad_x[f, i, rows] = value

        stream_derivative(sources[f], halo_lo.at[f], halo_hi.at[f], emit)

    prim_x(2)
    prim_x(0)

    def extras(x, carry):
        pack(cross_send, 0, x, grad_x[2, x])
        pack(cross_send, 1, x, grad_x[0, x])
        return carry

    lax.fori_loop(0, CX, extras, 0)
    a2a_start(2, cross_send, cross_recv)

    def build(fields):
        def body(s, carry):
            after = lax.rem(s + 1, GY)
            near_rows = pl.ds(pl.multiple_of(s * HZ, HZ), HZ)
            far_rows = pl.ds(pl.multiple_of(NZ // 2 + s * HZ, HZ), HZ)
            for column, fetch in fields:
                columns = pl.ds(column * NY, NY)
                here = fetch(s)
                other = pltpu.roll(jnp.where(low_lanes, fetch(after), here), NY // 2, axis=1)
                high, low = split(here)
                rhs_h[near_rows, columns] = high
                rhs_l[near_rows, columns] = low
                high, low = split(other)
                rhs_h[far_rows, columns] = high
                rhs_l[far_rows, columns] = low
            return carry

        lax.fori_loop(0, GY, body, 0, unroll=2)

    def span_product(start, count):
        columns = pl.ds(start * NY, count * NY)
        high = rhs_h[:, columns]
        product = jnp.dot(dh[...], high, preferred_element_type=jnp.float32)
        product += jnp.dot(dh[...], rhs_l[:, columns], preferred_element_type=jnp.float32)
        product += jnp.dot(dl[...], high, preferred_element_type=jnp.float32)
        return [
            product[:, f * NY : (f + 1) * NY].reshape(GY, HZ, NY) for f in range(count)
        ]

    for copy in loads[4:]:
        copy.wait()
    def half_pitch_derivative(fetch, slot):
        def body(s, carry):
            rows = pl.ds(pl.multiple_of(s * HZ, HZ), HZ)
            for side, value in enumerate((fetch(s), sib_value[slot, s])):
                high, low = split(value)
                span_in[0, rows, side * NY : (side + 1) * NY] = high
                span_in[1, rows, side * NY : (side + 1) * NY] = low
            return carry

        lax.fori_loop(0, GY, body, 0, unroll=2)
        product = jnp.dot(span_in[0], ys[...], preferred_element_type=jnp.float32)
        rest = jnp.dot(span_in[1], ys[:, :NY], preferred_element_type=jnp.float32)
        return (product[:, :NY] + product[:, NY:] + rest).reshape(GY, HZ, NY)

    a2a_wait_recv(0, speed_send, speed_recv)
    siblings = [sibling_copy(speed_recv.at[:, 1], 0), sibling_copy(state_recv.at[:, 0], 1)]
    siblings += [sibling_copy(sib_send_buf.at[f], 2 + f) for f in range(2)]
    siblings[0].start()
    build([(0, lambda s: speed_recv[s, 0]), (1, lambda s: speed_recv[s, 1])])
    for f, value in enumerate(span_product(0, 2)):
        slope_send[:, f] = value
    a2a_start(3, slope_send, slope_recv)

    a2a_wait_recv(1, state_send, state_recv)
    siblings[1].start()

    def span_first(s, carry):
        span_x[0, s] = state_recv[s, 1] * speed_recv[s, 1]
        span_visc[s] = viscosity(state_recv[s, 2])
        return carry

    lax.fori_loop(0, GY, span_first, 0, unroll=2)
    build([(2, lambda s: state_recv[s, 0]), (3, lambda s: span_x[0, s])])
    slopes = span_product(2, 2)
    dz_v2[...] = slopes[0]
    slope2_send[:, 0] = slopes[1]
    a2a_start(4, slope2_send, slope2_recv)

    siblings[0].wait_recv()
    span_dy[0] = half_pitch_derivative(lambda s: speed_recv[s, 1], 0)

    def shear(s, carry):
        s23 = span_visc[s] * (dz_v2[s] + span_dy[0, s])
        sib_send_buf[0, s] = s23
        sib_send_buf[1, s] = s23 * speed_recv[s, 1]
        return carry

    lax.fori_loop(0, GY, shear, 0, unroll=2)
    for copy in siblings[2:]:
        copy.start()
    siblings[1].wait_recv()
    span_dy[1] = half_pitch_derivative(lambda s: state_recv[s, 0], 1)
    build([(4, lambda s: state_recv[s, 2])])
    dz_t[...] = span_product(4, 1)[0]

    for f in range(2):
        siblings[2 + f].wait_recv()
        span_dy[2 + f] = half_pitch_derivative(lambda s, f=f: sib_send_buf[f, s], 2 + f)

    prim_x(1)
    prim_x(3)

    a2a_wait_recv(2, cross_send, cross_recv)

    def span_second(s, carry):
        v1, v3 = speed_recv[s, 0], speed_recv[s, 1]
        v2, density, temperature = [state_recv[s, f] for f in range(3)]
        m3 = span_x[0, s]
        pressure = temperature * density
        enthalpy = (heat_ratio / (heat_ratio - 1.0)) * pressure + 0.5 * density * (
            v1 * v1 + v2 * v2 + v3 * v3
        )
        dz1, dz3 = slope_send[s, 0], slope_send[s, 1]
        dx3, plane = cross_recv[s, 0], cross_recv[s, 1] + span_dy[1, s]
        visc = span_visc[s]
        s13 = visc * (dz1 + dx3)
        s23 = sib_send_buf[0, s]
        s33 = visc * (2.0 * dz3 - (2.0 / 3.0) * (plane + dz3))
        work = s13 * v1 + s23 * v2 + s33 * v3
        span_x[1, s] = m3 * v1 - s13
        span_x[2, s] = m3 * v2 - s23
        span_x[3, s] = m3 * v3 - s33 + pressure
        span_x[4, s] = enthalpy * v3 - work - (visc * conduction) * dz_t[s]
        return carry

    lax.fori_loop(0, GY, span_second, 0, unroll=2)
    build([(5 + f, lambda s, f=f: span_x[1 + f, s]) for f in range(4)])
    for pair in (0, 2):
        for f, value in enumerate(span_product(5 + pair, 2)):
            div_send[:, pair + f] = value - span_dy[pair + f] if pair else value
    a2a_start(5, div_send, div_recv)

    a2a_wait_recv(3, slope_send, slope_recv)

    def stream_flux(x, carry):
        dz1, dz3 = unpack(slope_recv, 0, x), unpack(slope_recv, 1, x)
        density, m1, m2, m3, energy = [con[f, x] for f in range(5)]
        v1, v2, v3, temperature = [prim[f, x] for f in range(4)]
        pressure = temperature * density
        dx1, dx2, dx3, dxt = [grad_x[f, x] for f in range(4)]
        visc = keep[0, x]
        bulk = (2.0 / 3.0) * (dx1 + grad_y[1, x] + dz3)
        s11 = visc * (2.0 * dx1 - bulk)
        s12 = visc * (dx2 + grad_y[0, x])
        s13 = visc * (dx3 + dz1)
        flux_x[0, x] = m1 * v1 + pressure - s11
        flux_x[1, x] = m2 * v1 - s12
        flux_x[2, x] = m3 * v1 - s13
        work = s11 * v1 + s12 * v2 + s13 * v3
        flux_x[3, x] = (energy + pressure) * v1 - work - (visc * conduction) * dxt
        keep[1, x] = bulk
        keep[2, x] = s12
        return carry

    lax.fori_loop(0, CX, stream_flux, 0)
    flux_halos = [halo_pair(flux_lo.at[f], flux_hi.at[f], 5 + f) for f in range(4)]
    for f in range(4):
        edge_store(flux_x.at[f], 5 + f)
        for copy in flux_halos[f]:
            copy.start()

    a2a_wait_recv(4, slope2_send, slope2_recv)

    def pitch_flux(x, carry):
        out_ref[0, x] = unpack(slope2_recv, 0, x)
        density, m1, m2, m3, energy = [con[f, x] for f in range(5)]
        v1, v2, v3, temperature = [prim[f, x] for f in range(4)]
        pressure = temperature * density
        visc, bulk, s12 = [keep[f, x] for f in range(3)]
        s22 = visc * (2.0 * grad_y[1, x] - bulk)
        work = s12 * v1 + s22 * v2
        pitch_store(0, x, m2)
        pitch_store(1, x, m1 * v2 - s12)
        pitch_store(2, x, m2 * v2 + pressure - s22)
        pitch_store(3, x, m3 * v2)
        flux = (energy + pressure) * v2 - work - (visc * conduction) * grad_y[3, x]
        pitch_store(4, x, flux)
        return carry

    lax.fori_loop(0, CX, pitch_flux, 0)
    out_ref[0] += pitch_derivative(0)
    for f in range(1, 5):
        out_ref[f] = pitch_derivative(f)

    def accumulate(f, own, lo, hi):
        def emit(i, rows, value):
            out_ref[f, i, rows] += value

        stream_derivative(own, lo, hi, emit)

    halo_wait(halos[4])
    accumulate(0, con.at[1], halo_lo.at[4], halo_hi.at[4])
    for f in range(4):
        halo_wait(flux_halos[f])
        accumulate(1 + f, flux_x.at[f], flux_lo.at[f], flux_hi.at[f])

    a2a_wait_recv(5, div_send, div_recv)

    def last(x, carry):
        for f in range(4):
            out_ref[1 + f, x] += unpack(div_recv, f, x)
        return carry

    lax.fori_loop(0, CX, last, 0)

    a2a_wait_send(0, speed_send, speed_recv)
    a2a_wait_send(1, state_send, state_recv)
    a2a_wait_send(2, cross_send, cross_recv)
    a2a_wait_send(3, slope_send, slope_recv)
    a2a_wait_send(4, slope2_send, slope2_recv)
    a2a_wait_send(5, div_send, div_recv)
    for copy in siblings:
        copy.wait_send()
    for copies in halos + flux_halos:
        for copy in copies:
            copy.wait_send()


def per_device(mass_per_volume, momentum, energy):
    dh, dl = span_operand()
    yc = pitch_operand()
    f32, bf16 = jnp.float32, jnp.bfloat16
    field = (CX, ZB, NY)
    piece = (HZ, NY)
    spread, conserved = pl.pallas_call(
        kernel,
        out_shape=[jax.ShapeDtypeStruct((5,) + field, f32)] * 2,
        in_specs=[pl.BlockSpec(memory_space=pltpu.HBM)] * 7,
        out_specs=[pl.BlockSpec(memory_space=pltpu.VMEM)] * 2,
        scratch_shapes=[
            pltpu.VMEM((NZ // 2, NZ), bf16),
            pltpu.VMEM((NZ // 2, NZ), bf16),
            pltpu.VMEM((2 * NY, 2 * NY), bf16),
            pltpu.VMEM((2 * NY, 2 * NY), bf16),
            pltpu.VMEM((4,) + field, f32),
            pltpu.VMEM((9, 2, EDGE, ZB, NY), f32),
            pltpu.VMEM((5, EDGE, ZB, NY), f32),
            pltpu.VMEM((5, EDGE, ZB, NY), f32),
            pltpu.VMEM((4, EDGE, ZB, NY), f32),
            pltpu.VMEM((4, EDGE, ZB, NY), f32),
        ]
        + [pltpu.VMEM((GY, n) + piece, f32) for n in (2, 3, 2, 2, 1, 4) for _ in range(2)]
        + [
            pltpu.VMEM((4,) + field, f32),
            pltpu.VMEM((4,) + field, f32),
            pltpu.VMEM((4,) + field, f32),
            pltpu.VMEM((3,) + field, f32),
            pltpu.VMEM((5, CX * ZB, 2 * NY), bf16),
            pltpu.VMEM((5, GY) + piece, f32),
            pltpu.VMEM((NZ, 9 * NY), bf16),
            pltpu.VMEM((NZ, 9 * NY), bf16),
            pltpu.VMEM((GY,) + piece, f32),
            pltpu.VMEM((GY,) + piece, f32),
            pltpu.VMEM((4, GY) + piece, f32),
            pltpu.VMEM((2, GY) + piece, f32),
            pltpu.VMEM((2, NZ // 2, 2 * NY), bf16),
            pltpu.VMEM((4, GY) + piece, f32),
            pltpu.VMEM((GY,) + piece, f32),
            pltpu.SemaphoreType.DMA((4,)),
            pltpu.SemaphoreType.DMA((4,)),
            pltpu.SemaphoreType.DMA((7,)),
            pltpu.SemaphoreType.DMA((6, GY - 1)),
            pltpu.SemaphoreType.DMA((6, GY - 1)),
            pltpu.SemaphoreType.DMA((2, 9)),
            pltpu.SemaphoreType.DMA((2, 9)),
        ],
        compiler_params=pltpu.CompilerParams(
            collective_id=0, has_side_effects=True, vmem_limit_bytes=24 * 1024 * 1024
        ),
    )(*[pltpu.with_memory_space_constraint(x, pltpu.HBM) for x in (mass_per_volume, momentum, energy, jnp.asarray(dh), jnp.asarray(dl), jnp.asarray(yc), jnp.asarray(half_pitch_operand()))])
    tendency = -spread
    return tendency, conserved + section_step * tendency


def solution(mesh):
    in_specs = (P("gx", "gy", None), P(None, "gx", "gy", None), P("gx", "gy", None))
    out_specs = (P(None, "gx", "gy", None), P(None, "gx", "gy", None))
    return jax.shard_map(
        per_device, mesh=mesh, in_specs=in_specs, out_specs=out_specs, check_vma=False
    )
```

```python
import jax
import jax.numpy as jnp
import ml_dtypes
import numpy as np
from jax import lax
from jax.experimental import pallas as pl
from jax.experimental.pallas import tpu as pltpu
from jax.sharding import PartitionSpec as P

CX = 8
CY = 8
NZ = 512
NY = 128
HALO = 4
GY = 16
ZB = NZ // GY
HZ = ZB // 2
MESH = pl.DeviceIdType.MESH

heat_ratio = 1.4
shear_resistance_reference = 0.08
sutherland_power_law = 0.7
prandtl = 0.72
section_step = 0.05
compact_alpha = 1.0 / 3.0
compact_near = 14.0 / 9.0
compact_far = 1.0 / 9.0
conduction = heat_ratio / ((heat_ratio - 1.0) * prandtl)


def tridiagonal_inverse_product(length, stencil):
    solved = np.array(stencil)
    upper_ratio = np.zeros(length)
    for row_index in range(length):
        if row_index == 0:
            pivot_value = 1.0
            solved[row_index] = solved[row_index] / pivot_value
        else:
            pivot_value = 1.0 - compact_alpha * upper_ratio[row_index - 1]
            solved[row_index] = (
                solved[row_index] - compact_alpha * solved[row_index - 1]
            ) / pivot_value
        upper_ratio[row_index] = compact_alpha / pivot_value
    for row_index in range(length - 2, -1, -1):
        solved[row_index] = solved[row_index] - upper_ratio[row_index] * solved[row_index + 1]
    return solved


def compact_matrix(block_size, margin):
    length = block_size + 2 * margin
    stencil = compact_near / 2.0 * (np.eye(length, k=1) - np.eye(length, k=-1))
    stencil = stencil + compact_far / 4.0 * (np.eye(length, k=2) - np.eye(length, k=-2))
    inverse_product = tridiagonal_inverse_product(length, stencil)
    return inverse_product[margin : margin + block_size]


def pitch_matrix(total, block_size):
    matrix = compact_matrix(block_size, HALO)
    result = np.zeros((total, total))
    rows_all = np.arange(total)
    block_start = rows_all // block_size * block_size
    for offset in range(block_size + 2 * HALO):
        columns = (block_start - HALO + offset) % total
        result[rows_all, columns] += matrix[rows_all % block_size, offset]
    return result


def span_kernel(offsets, total):
    angles = np.pi * offsets / total
    signs = np.where(offsets % 2 == 0, 1.0, -1.0)
    zero = offsets % total == 0
    sines = np.where(zero, 1.0, np.sin(angles))
    return np.where(zero, 0.0, np.pi / total * signs * np.cos(angles) / sines)


def high_low(matrix):
    high = matrix.astype(ml_dtypes.bfloat16)
    low = (matrix - high.astype(np.float64)).astype(ml_dtypes.bfloat16)
    return high, low


def span_operand():
    z = (np.arange(GY)[:, None] * ZB + np.arange(HZ)[None, :]).reshape(-1)
    near = span_kernel(z[:, None] - z[None, :], NZ)
    far = span_kernel(z[:, None] - (z[None, :] + HZ), NZ)
    return high_low(np.concatenate([near, far], 1))


def pitch_operand():
    high, low = high_low(pitch_matrix(NY, CY).T)
    top = np.concatenate([high, low], 1)
    bottom = np.concatenate([high, np.zeros_like(low)], 1)
    return np.concatenate([top, bottom], 0)


def half_pitch_operand():
    matrix = pitch_matrix(NY, CY).T
    half = NY // 2
    near, far = matrix[:half, :half], matrix[half:, :half]
    assert np.allclose(near, matrix[half:, half:]) and np.allclose(far, matrix[:half, half:])
    stacked = np.concatenate([np.kron(np.eye(2), near), np.kron(np.eye(2), far)], 0)
    return np.concatenate(high_low(stacked), 1)


MATRIX_X = compact_matrix(CX, HALO)
EDGE = HALO - 1
OUTERMOST = float(MATRIX_X[0, 0] / MATRIX_X[0, 1])
assert np.allclose(MATRIX_X[:, 0], OUTERMOST * MATRIX_X[:, 1], rtol=1e-9, atol=1e-12)
SEGMENT = CX + 2 * EDGE
MATRIX_E = MATRIX_X[:, 1:-1]


def split(value):
    high = value.astype(jnp.bfloat16)
    return high, (value - high.astype(jnp.float32)).astype(jnp.bfloat16)


def compact_rows(segment):
    half, end = SEGMENT // 2, SEGMENT - 1
    even = [segment[i] + segment[end - i] for i in range(half)]
    odd = [segment[i] - segment[end - i] for i in range(half)]
    result = [None] * CX
    for i in range(CX // 2):
        row = MATRIX_E[i]
        both = sum(float(0.5 * (row[j] - row[end - j])) * odd[j] for j in range(half))
        diff = sum(float(0.5 * (row[j] + row[end - j])) * even[j] for j in range(half))
        result[i] = both + diff
        result[CX - 1 - i] = both - diff
    return result


def exchange_halves(top, bottom, low_lanes):
    moved = pltpu.roll(jnp.where(low_lanes, bottom, top), NY // 2, axis=1)
    return jnp.where(low_lanes, top, moved), jnp.where(low_lanes, moved, bottom)


def viscosity(temperature):
    return shear_resistance_reference * jnp.exp(sutherland_power_law * jnp.log(temperature))


RUN = 16
RELAYED = (1, 3, 4, 7, 8)
STEPS = [
    (dx, dy, dc)
    for dc in range(2)
    for dx, dy in ((2, 1), (1, 1), (3, 1), (2, 0), (0, 1), (1, 0), (3, 0))
] + [(0, 0, 1)]


def kernel(
    rho_hbm, mom_hbm, en_hbm, dh_hbm, dl_hbm, yc_hbm, ys_hbm, out_ref, con,
    dh, dl, yc, ys, prim, edges, halo_lo, halo_hi, flux_lo, flux_hi,
    speed_send, speed_recv, state_send, state_recv, cross_send, cross_recv,
    slope_send, slope_recv, slope2_send, slope2_recv, div_send, div_recv,
    grad_x, grad_y, flux_x, keep, pitch_in, span_x, rhs_h, rhs_l, dz_t, span_visc,
    sib_value, sib_send_buf, span_in, span_dy, dz_v2, sib_send_sem, sib_recv_sem,
    load_sem, a2a_send_sem, a2a_recv_sem, halo_send_sem, halo_recv_sem, relay, relay_send_sem, relay_recv_sem,
):
    gx = lax.axis_index("gx")
    me = lax.axis_index("gy")
    n_gx = lax.axis_size("gx")
    right, left = lax.rem(gx + 1, n_gx), lax.rem(gx + n_gx - 1, n_gx)
    chip_x, chip_y, core = me // 4, lax.rem(me // 2, 2), lax.rem(me, 2)
    partners = [
        lax.rem(chip_x + dx, 4) * 4 + lax.rem(chip_y + dy, 2) * 2 + lax.rem(core + dc, 2)
        for dx, dy, dc in STEPS
    ]

    loads = [
        pltpu.make_async_copy(rho_hbm, con.at[0], load_sem.at[0]),
        pltpu.make_async_copy(mom_hbm, con.at[pl.ds(1, 3)], load_sem.at[1]),
        pltpu.make_async_copy(en_hbm, con.at[4], load_sem.at[2]),
        pltpu.make_async_copy(yc_hbm, yc, load_sem.at[3]),
        pltpu.make_async_copy(dh_hbm, dh, load_sem.at[4]),
        pltpu.make_async_copy(dl_hbm, dl, load_sem.at[5]),
        pltpu.make_async_copy(ys_hbm, ys, load_sem.at[6]),
    ]
    for copy in loads:
        copy.start()

    barrier = pltpu.get_barrier_semaphore()
    sibling = partners[-1]
    for partner in partners:
        pl.semaphore_signal(barrier, inc=1, device_id={"gy": partner}, device_id_type=MESH)
    for neighbour in (left, right):
        pl.semaphore_signal(barrier, inc=1, device_id={"gx": neighbour}, device_id_type=MESH)

    run = lax.rem(gx, RUN)
    first_in_run, last_in_run = run == 0, run == RUN - 1
    relays_up, relays_down = run == 1, run == RUN - 2
    beyond_right, beyond_left = lax.rem(gx + 2, n_gx), lax.rem(gx + n_gx - 2, n_gx)
    for condition, source in ((relays_up, beyond_left), (relays_down, beyond_right)):

        @pl.when(condition)
        def _(source=source):
            pl.semaphore_signal(barrier, inc=1, device_id={"gx": source}, device_id_type=MESH)

    low_lanes = lax.broadcasted_iota(jnp.int32, (HZ, NY), 1) < NY // 2

    def a2a(phase, send, recv, step, partner):
        return pltpu.make_async_remote_copy(
            src_ref=send.at[partner],
            dst_ref=recv.at[me],
            send_sem=a2a_send_sem.at[phase, step],
            recv_sem=a2a_recv_sem.at[phase, step],
            device_id={"gy": partner},
            device_id_type=MESH,
        )

    def a2a_start(phase, send, recv):
        for step, partner in enumerate(partners):
            a2a(phase, send, recv, step, partner).start()
        recv[me] = send[me]

    def a2a_wait_recv(phase, send, recv):
        def body(step, carry):
            a2a(phase, send, recv, step, partners[0]).wait_recv()
            return carry

        lax.fori_loop(0, GY - 1, body, 0)

    def a2a_wait_send(phase, send, recv):
        def body(step, carry):
            a2a(phase, send, recv, step, partners[0]).wait_send()
            return carry

        lax.fori_loop(0, GY - 1, body, 0)

    def halo_pair(lo, hi, slot):
        up = pltpu.make_async_remote_copy(
            src_ref=edges.at[slot, 0], dst_ref=lo,
            send_sem=halo_send_sem.at[0, slot], recv_sem=halo_recv_sem.at[0, slot],
            device_id={"gx": right}, device_id_type=MESH,
        )
        down = pltpu.make_async_remote_copy(
            src_ref=edges.at[slot, 1], dst_ref=hi,
            send_sem=halo_send_sem.at[1, slot], recv_sem=halo_recv_sem.at[1, slot],
            device_id={"gx": left}, device_id_type=MESH,
        )
        return up, down

    def halo_start(pair, slot):
        sides = ((pair[0], last_in_run, beyond_right), (pair[1], first_in_run, beyond_left))
        for side, (copy, at_end, target) in enumerate(sides):
            if slot not in RELAYED:
                copy.start()
                continue

            @pl.when(jnp.logical_not(at_end))
            def _(copy=copy):
                copy.start()

            @pl.when(at_end)
            def _(side=side, target=target):
                pltpu.make_async_remote_copy(
                    src_ref=edges.at[slot, side], dst_ref=relay.at[RELAYED.index(slot)],
                    send_sem=halo_send_sem.at[side, slot],
                    recv_sem=relay_recv_sem.at[RELAYED.index(slot)],
                    device_id={"gx": target}, device_id_type=MESH,
                ).start()

    def relay_copies(slot, lo, hi):
        index = RELAYED.index(slot)
        return [
            (
                condition,
                pltpu.make_async_remote_copy(
                    src_ref=relay.at[index], dst_ref=target,
                    send_sem=relay_send_sem.at[index], recv_sem=halo_recv_sem.at[side, slot],
                    device_id={"gx": neighbour}, device_id_type=MESH,
                ),
                pltpu.make_async_remote_copy(
                    src_ref=relay.at[index], dst_ref=relay.at[index],
                    send_sem=relay_send_sem.at[index], recv_sem=relay_recv_sem.at[index],
                    device_id={"gx": neighbour}, device_id_type=MESH,
                ),
            )
            for side, condition, target, neighbour in (
                (0, relays_up, lo, left),
                (1, relays_down, hi, right),
            )
        ]

    def relay_start(copies):
        for condition, forward, arrival in copies:

            @pl.when(condition)
            def _(forward=forward, arrival=arrival):
                arrival.wait_recv()
                forward.start()

    def edge_store(source, slot):
        edges[slot, 0, 0] = source[CX - 3] + OUTERMOST * source[CX - 4]
        edges[slot, 0, 1] = source[CX - 2]
        edges[slot, 0, 2] = source[CX - 1]
        edges[slot, 1, 0] = source[0]
        edges[slot, 1, 1] = source[1]
        edges[slot, 1, 2] = source[2] + OUTERMOST * source[3]

    def sibling_copy(source, slot):
        return pltpu.make_async_remote_copy(
            src_ref=source, dst_ref=sib_value.at[slot],
            send_sem=sib_send_sem.at[slot], recv_sem=sib_recv_sem.at[slot],
            device_id={"gy": sibling}, device_id_type=MESH,
        )

    def pack(send, slot, x, value):
        p0, p1 = exchange_halves(value[:HZ], value[HZ:], low_lanes)
        send[2 * x, slot] = p0
        send[2 * x + 1, slot] = p1

    def unpack(recv, slot, x):
        top, bottom = exchange_halves(recv[2 * x, slot], recv[2 * x + 1, slot], low_lanes)
        return jnp.concatenate([top, bottom], 0)

    def pitch_store(f, x, value):
        high, low = split(value)
        rows = pl.ds(pl.multiple_of(x * ZB, ZB), ZB)
        pitch_in[f, rows, :NY] = high
        pitch_in[f, rows, NY:] = low

    for copy in loads[:3]:
        copy.wait()

    def first(x, carry):
        density, m1, m2, m3, energy = [con[f, x] for f in range(5)]
        inverse = 1.0 / density
        v1, v2, v3 = m1 * inverse, m2 * inverse, m3 * inverse
        kinetic = 0.5 * (m1 * v1 + m2 * v2 + m3 * v3)
        temperature = (heat_ratio - 1.0) * (energy - kinetic) * inverse
        pack(speed_send, 0, x, v1)
        pack(speed_send, 1, x, v3)
        pack(state_send, 0, x, v2)
        pack(state_send, 1, x, density)
        pack(state_send, 2, x, temperature)
        for f, value in enumerate((v1, v2, v3, temperature)):
            prim[f, x] = value
            pitch_store(f, x, value)
        keep[0, x] = viscosity(temperature)
        return carry

    lax.fori_loop(0, CX, first, 0)

    sources = [prim.at[0], prim.at[1], prim.at[2], prim.at[3], con.at[1]]
    for f in range(5):
        edge_store(sources[f], f)

    at_end = jnp.logical_or(first_in_run, last_in_run)

    @pl.when(at_end)
    def _():
        pl.semaphore_wait(barrier, GY + 2)

    @pl.when(jnp.logical_not(at_end))
    def _():
        pl.semaphore_wait(barrier, GY + 1)

    halos = [halo_pair(halo_lo.at[f], halo_hi.at[f], f) for f in range(5)]
    for f in (2, 0):
        halo_start(halos[f], f)
    a2a_start(0, speed_send, speed_recv)
    a2a_start(1, state_send, state_recv)

    for f in (1, 3, 4):
        halo_start(halos[f], f)

    loads[3].wait()

    def pitch_derivative(f):
        product = jnp.dot(pitch_in[f], yc[...], preferred_element_type=jnp.float32)
        return (product[:, :NY] + product[:, NY:]).reshape(CX, ZB, NY)

    for f in (0, 1, 3):
        grad_y[f] = pitch_derivative(f)

    def stream_derivative(own, lo, hi, emit):
        def body(t, carry):
            rows = pl.ds(pl.multiple_of(t * 8, 8), 8)
            segment = [lo[i, rows] for i in range(EDGE)]
            segment += [own[i, rows] for i in range(CX)]
            segment += [hi[i, rows] for i in range(EDGE)]
            for i, value in enumerate(compact_rows(segment)):
                emit(i, rows, value)
            return carry

        lax.fori_loop(0, ZB // 8, body, 0)

    def halo_wait(copies):
        for copy in copies:
            copy.wait_recv()

    def prim_x(f):
        halo_wait(halos[f])

        def emit(i, rows, value):
            grad_x[f, i, rows] = value

        stream_derivative(sources[f], halo_lo.at[f], halo_hi.at[f], emit)

    prim_x(2)
    prim_x(0)

    def extras(x, carry):
        pack(cross_send, 0, x, grad_x[2, x])
        pack(cross_send, 1, x, grad_x[0, x])
        return carry

    lax.fori_loop(0, CX, extras, 0)
    a2a_start(2, cross_send, cross_recv)
    relays = [relay_copies(f, halo_lo.at[f], halo_hi.at[f]) for f in (1, 3, 4)]
    for copies in relays:
        relay_start(copies)

    def build(fields):
        def body(s, carry):
            after = lax.rem(s + 1, GY)
            near_rows = pl.ds(pl.multiple_of(s * HZ, HZ), HZ)
            far_rows = pl.ds(pl.multiple_of(NZ // 2 + s * HZ, HZ), HZ)
            for column, fetch in fields:
                columns = pl.ds(column * NY, NY)
                here = fetch(s)
                other = pltpu.roll(jnp.where(low_lanes, fetch(after), here), NY // 2, axis=1)
                high, low = split(here)
                rhs_h[near_rows, columns] = high
                rhs_l[near_rows, columns] = low
                high, low = split(other)
                rhs_h[far_rows, columns] = high
                rhs_l[far_rows, columns] = low
            return carry

        lax.fori_loop(0, GY, body, 0, unroll=2)

    def span_product(start, count):
        columns = pl.ds(start * NY, count * NY)
        high = rhs_h[:, columns]
        product = jnp.dot(dh[...], high, preferred_element_type=jnp.float32)
        product += jnp.dot(dh[...], rhs_l[:, columns], preferred_element_type=jnp.float32)
        product += jnp.dot(dl[...], high, preferred_element_type=jnp.float32)
        return [
            product[:, f * NY : (f + 1) * NY].reshape(GY, HZ, NY) for f in range(count)
        ]

    for copy in loads[4:]:
        copy.wait()
    def half_pitch_derivative(fetch, slot):
        def body(s, carry):
            rows = pl.ds(pl.multiple_of(s * HZ, HZ), HZ)
            for side, value in enumerate((fetch(s), sib_value[slot, s])):
                high, low = split(value)
                span_in[0, rows, side * NY : (side + 1) * NY] = high
                span_in[1, rows, side * NY : (side + 1) * NY] = low
            return carry

        lax.fori_loop(0, GY, body, 0, unroll=2)
        product = jnp.dot(span_in[0], ys[...], preferred_element_type=jnp.float32)
        rest = jnp.dot(span_in[1], ys[:, :NY], preferred_element_type=jnp.float32)
        return (product[:, :NY] + product[:, NY:] + rest).reshape(GY, HZ, NY)

    a2a_wait_recv(0, speed_send, speed_recv)
    siblings = [sibling_copy(speed_recv.at[:, 1], 0), sibling_copy(state_recv.at[:, 0], 1)]
    siblings += [sibling_copy(sib_send_buf.at[f], 2 + f) for f in range(2)]
    siblings[0].start()
    build([(0, lambda s: speed_recv[s, 0]), (1, lambda s: speed_recv[s, 1])])
    for f, value in enumerate(span_product(0, 2)):
        slope_send[:, f] = value
    a2a_start(3, slope_send, slope_recv)

    a2a_wait_recv(1, state_send, state_recv)
    siblings[1].start()

    def span_first(s, carry):
        span_x[0, s] = state_recv[s, 1] * speed_recv[s, 1]
        span_visc[s] = viscosity(state_recv[s, 2])
        return carry

    lax.fori_loop(0, GY, span_first, 0, unroll=2)
    build([(2, lambda s: state_recv[s, 0]), (3, lambda s: span_x[0, s])])
    slopes = span_product(2, 2)
    dz_v2[...] = slopes[0]
    slope2_send[:, 0] = slopes[1]
    a2a_start(4, slope2_send, slope2_recv)

    siblings[0].wait_recv()
    span_dy[0] = half_pitch_derivative(lambda s: speed_recv[s, 1], 0)

    def shear(s, carry):
        s23 = span_visc[s] * (dz_v2[s] + span_dy[0, s])
        sib_send_buf[0, s] = s23
        sib_send_buf[1, s] = s23 * speed_recv[s, 1]
        return carry

    lax.fori_loop(0, GY, shear, 0, unroll=2)
    for copy in siblings[2:]:
        copy.start()
    siblings[1].wait_recv()
    span_dy[1] = half_pitch_derivative(lambda s: state_recv[s, 0], 1)
    build([(4, lambda s: state_recv[s, 2])])
    dz_t[...] = span_product(4, 1)[0]

    for f in range(2):
        siblings[2 + f].wait_recv()
        span_dy[2 + f] = half_pitch_derivative(lambda s, f=f: sib_send_buf[f, s], 2 + f)

    prim_x(1)
    prim_x(3)

    a2a_wait_recv(2, cross_send, cross_recv)

    def span_second(s, carry):
        v1, v3 = speed_recv[s, 0], speed_recv[s, 1]
        v2, density, temperature = [state_recv[s, f] for f in range(3)]
        m3 = span_x[0, s]
        pressure = temperature * density
        enthalpy = (heat_ratio / (heat_ratio - 1.0)) * pressure + 0.5 * density * (
            v1 * v1 + v2 * v2 + v3 * v3
        )
        dz1, dz3 = slope_send[s, 0], slope_send[s, 1]
        dx3, plane = cross_recv[s, 0], cross_recv[s, 1] + span_dy[1, s]
        visc = span_visc[s]
        s13 = visc * (dz1 + dx3)
        s23 = sib_send_buf[0, s]
        s33 = visc * (2.0 * dz3 - (2.0 / 3.0) * (plane + dz3))
        work = s13 * v1 + s23 * v2 + s33 * v3
        span_x[1, s] = m3 * v1 - s13
        span_x[2, s] = m3 * v2 - s23
        span_x[3, s] = m3 * v3 - s33 + pressure
        span_x[4, s] = enthalpy * v3 - work - (visc * conduction) * dz_t[s]
        return carry

    lax.fori_loop(0, GY, span_second, 0, unroll=2)
    build([(5 + f, lambda s, f=f: span_x[1 + f, s]) for f in range(4)])
    for pair in (0, 2):
        for f, value in enumerate(span_product(5 + pair, 2)):
            div_send[:, pair + f] = value - span_dy[pair + f] if pair else value
    a2a_start(5, div_send, div_recv)

    a2a_wait_recv(3, slope_send, slope_recv)

    def stream_flux(x, carry):
        dz1, dz3 = unpack(slope_recv, 0, x), unpack(slope_recv, 1, x)
        density, m1, m2, m3, energy = [con[f, x] for f in range(5)]
        v1, v2, v3, temperature = [prim[f, x] for f in range(4)]
        pressure = temperature * density
        dx1, dx2, dx3, dxt = [grad_x[f, x] for f in range(4)]
        visc = keep[0, x]
        bulk = (2.0 / 3.0) * (dx1 + grad_y[1, x] + dz3)
        s11 = visc * (2.0 * dx1 - bulk)
        s12 = visc * (dx2 + grad_y[0, x])
        s13 = visc * (dx3 + dz1)
        flux_x[0, x] = m1 * v1 + pressure - s11
        flux_x[1, x] = m2 * v1 - s12
        flux_x[2, x] = m3 * v1 - s13
        work = s11 * v1 + s12 * v2 + s13 * v3
        flux_x[3, x] = (energy + pressure) * v1 - work - (visc * conduction) * dxt
        keep[1, x] = bulk
        keep[2, x] = s12
        return carry

    lax.fori_loop(0, CX, stream_flux, 0)
    flux_halos = [halo_pair(flux_lo.at[f], flux_hi.at[f], 5 + f) for f in range(4)]
    for f in range(4):
        edge_store(flux_x.at[f], 5 + f)
        halo_start(flux_halos[f], 5 + f)

    a2a_wait_recv(4, slope2_send, slope2_recv)

    def pitch_flux(x, carry):
        out_ref[0, x] = unpack(slope2_recv, 0, x)
        density, m1, m2, m3, energy = [con[f, x] for f in range(5)]
        v1, v2, v3, temperature = [prim[f, x] for f in range(4)]
        pressure = temperature * density
        visc, bulk, s12 = [keep[f, x] for f in range(3)]
        s22 = visc * (2.0 * grad_y[1, x] - bulk)
        work = s12 * v1 + s22 * v2
        pitch_store(0, x, m2)
        pitch_store(1, x, m1 * v2 - s12)
        pitch_store(2, x, m2 * v2 + pressure - s22)
        pitch_store(3, x, m3 * v2)
        flux = (energy + pressure) * v2 - work - (visc * conduction) * grad_y[3, x]
        pitch_store(4, x, flux)
        return carry

    lax.fori_loop(0, CX, pitch_flux, 0)
    out_ref[0] += pitch_derivative(0)
    for f in range(1, 5):
        out_ref[f] = pitch_derivative(f)

    relays += [relay_copies(5 + f, flux_lo.at[f], flux_hi.at[f]) for f in (2, 3)]
    for copies in relays[3:]:
        relay_start(copies)

    def accumulate(f, own, lo, hi):
        def emit(i, rows, value):
            out_ref[f, i, rows] += value

        stream_derivative(own, lo, hi, emit)

    halo_wait(halos[4])
    accumulate(0, con.at[1], halo_lo.at[4], halo_hi.at[4])
    for f in range(4):
        halo_wait(flux_halos[f])
        accumulate(1 + f, flux_x.at[f], flux_lo.at[f], flux_hi.at[f])

    a2a_wait_recv(5, div_send, div_recv)

    def last(x, carry):
        for f in range(4):
            out_ref[1 + f, x] += unpack(div_recv, f, x)
        return carry

    lax.fori_loop(0, CX, last, 0)

    a2a_wait_send(0, speed_send, speed_recv)
    a2a_wait_send(1, state_send, state_recv)
    a2a_wait_send(2, cross_send, cross_recv)
    a2a_wait_send(3, slope_send, slope_recv)
    a2a_wait_send(4, slope2_send, slope2_recv)
    a2a_wait_send(5, div_send, div_recv)
    for copy in siblings:
        copy.wait_send()
    for copies in relays:
        for condition, forward, _ in copies:

            @pl.when(condition)
            def _(forward=forward):
                forward.wait_send()

    for copies in halos + flux_halos:
        for copy in copies:
            copy.wait_send()


def per_device(mass_per_volume, momentum, energy):
    dh, dl = span_operand()
    yc = pitch_operand()
    f32, bf16 = jnp.float32, jnp.bfloat16
    field = (CX, ZB, NY)
    piece = (HZ, NY)
    spread, conserved = pl.pallas_call(
        kernel,
        out_shape=[jax.ShapeDtypeStruct((5,) + field, f32)] * 2,
        in_specs=[pl.BlockSpec(memory_space=pltpu.HBM)] * 7,
        out_specs=[pl.BlockSpec(memory_space=pltpu.VMEM)] * 2,
        scratch_shapes=[
            pltpu.VMEM((NZ // 2, NZ), bf16),
            pltpu.VMEM((NZ // 2, NZ), bf16),
            pltpu.VMEM((2 * NY, 2 * NY), bf16),
            pltpu.VMEM((2 * NY, 2 * NY), bf16),
            pltpu.VMEM((4,) + field, f32),
            pltpu.VMEM((9, 2, EDGE, ZB, NY), f32),
            pltpu.VMEM((5, EDGE, ZB, NY), f32),
            pltpu.VMEM((5, EDGE, ZB, NY), f32),
            pltpu.VMEM((4, EDGE, ZB, NY), f32),
            pltpu.VMEM((4, EDGE, ZB, NY), f32),
        ]
        + [pltpu.VMEM((GY, n) + piece, f32) for n in (2, 3, 2, 2, 1, 4) for _ in range(2)]
        + [
            pltpu.VMEM((4,) + field, f32),
            pltpu.VMEM((4,) + field, f32),
            pltpu.VMEM((4,) + field, f32),
            pltpu.VMEM((3,) + field, f32),
            pltpu.VMEM((5, CX * ZB, 2 * NY), bf16),
            pltpu.VMEM((5, GY) + piece, f32),
            pltpu.VMEM((NZ, 9 * NY), bf16),
            pltpu.VMEM((NZ, 9 * NY), bf16),
            pltpu.VMEM((GY,) + piece, f32),
            pltpu.VMEM((GY,) + piece, f32),
            pltpu.VMEM((4, GY) + piece, f32),
            pltpu.VMEM((2, GY) + piece, f32),
            pltpu.VMEM((2, NZ // 2, 2 * NY), bf16),
            pltpu.VMEM((4, GY) + piece, f32),
            pltpu.VMEM((GY,) + piece, f32),
            pltpu.SemaphoreType.DMA((4,)),
            pltpu.SemaphoreType.DMA((4,)),
            pltpu.SemaphoreType.DMA((7,)),
            pltpu.SemaphoreType.DMA((6, GY - 1)),
            pltpu.SemaphoreType.DMA((6, GY - 1)),
            pltpu.SemaphoreType.DMA((2, 9)),
            pltpu.SemaphoreType.DMA((2, 9)),
            pltpu.VMEM((len(RELAYED), EDGE, ZB, NY), f32),
            pltpu.SemaphoreType.DMA((len(RELAYED),)),
            pltpu.SemaphoreType.DMA((len(RELAYED),)),
        ],
        compiler_params=pltpu.CompilerParams(
            collective_id=0, has_side_effects=True, vmem_limit_bytes=24 * 1024 * 1024
        ),
    )(*[pltpu.with_memory_space_constraint(x, pltpu.HBM) for x in (mass_per_volume, momentum, energy, jnp.asarray(dh), jnp.asarray(dl), jnp.asarray(yc), jnp.asarray(half_pitch_operand()))])
    tendency = -spread
    return tendency, conserved + section_step * tendency


def solution(mesh):
    in_specs = (P("gx", "gy", None), P(None, "gx", "gy", None), P("gx", "gy", None))
    out_specs = (P(None, "gx", "gy", None), P(None, "gx", "gy", None))
    return jax.shard_map(
        per_device, mesh=mesh, in_specs=in_specs, out_specs=out_specs, check_vma=False
    )
```

```python
import jax
import jax.numpy as jnp
import ml_dtypes
import numpy as np
from jax import lax
from jax.experimental import pallas as pl
from jax.experimental.pallas import tpu as pltpu
from jax.sharding import PartitionSpec as P

CX = 8
CY = 8
NZ = 512
NY = 128
HALO = 4
GY = 16
ZB = NZ // GY
HZ = ZB // 2
MESH = pl.DeviceIdType.MESH

heat_ratio = 1.4
shear_resistance_reference = 0.08
sutherland_power_law = 0.7
prandtl = 0.72
section_step = 0.05
compact_alpha = 1.0 / 3.0
compact_near = 14.0 / 9.0
compact_far = 1.0 / 9.0
conduction = heat_ratio / ((heat_ratio - 1.0) * prandtl)


def tridiagonal_inverse_product(length, stencil):
    solved = np.array(stencil)
    upper_ratio = np.zeros(length)
    for row_index in range(length):
        if row_index == 0:
            pivot_value = 1.0
            solved[row_index] = solved[row_index] / pivot_value
        else:
            pivot_value = 1.0 - compact_alpha * upper_ratio[row_index - 1]
            solved[row_index] = (
                solved[row_index] - compact_alpha * solved[row_index - 1]
            ) / pivot_value
        upper_ratio[row_index] = compact_alpha / pivot_value
    for row_index in range(length - 2, -1, -1):
        solved[row_index] = solved[row_index] - upper_ratio[row_index] * solved[row_index + 1]
    return solved


def compact_matrix(block_size, margin):
    length = block_size + 2 * margin
    stencil = compact_near / 2.0 * (np.eye(length, k=1) - np.eye(length, k=-1))
    stencil = stencil + compact_far / 4.0 * (np.eye(length, k=2) - np.eye(length, k=-2))
    inverse_product = tridiagonal_inverse_product(length, stencil)
    return inverse_product[margin : margin + block_size]


def pitch_matrix(total, block_size):
    matrix = compact_matrix(block_size, HALO)
    result = np.zeros((total, total))
    rows_all = np.arange(total)
    block_start = rows_all // block_size * block_size
    for offset in range(block_size + 2 * HALO):
        columns = (block_start - HALO + offset) % total
        result[rows_all, columns] += matrix[rows_all % block_size, offset]
    return result


def span_kernel(offsets, total):
    angles = np.pi * offsets / total
    signs = np.where(offsets % 2 == 0, 1.0, -1.0)
    zero = offsets % total == 0
    sines = np.where(zero, 1.0, np.sin(angles))
    return np.where(zero, 0.0, np.pi / total * signs * np.cos(angles) / sines)


def high_low(matrix):
    high = matrix.astype(ml_dtypes.bfloat16)
    low = (matrix - high.astype(np.float64)).astype(ml_dtypes.bfloat16)
    return high, low


def span_operand():
    z = (np.arange(GY)[:, None] * ZB + np.arange(HZ)[None, :]).reshape(-1)
    near = span_kernel(z[:, None] - z[None, :], NZ)
    far = span_kernel(z[:, None] - (z[None, :] + HZ), NZ)
    return high_low(np.concatenate([near, far], 1))


def pitch_operand():
    high, low = high_low(pitch_matrix(NY, CY).T)
    top = np.concatenate([high, low], 1)
    bottom = np.concatenate([high, np.zeros_like(low)], 1)
    return np.concatenate([top, bottom], 0)


def half_pitch_operand():
    matrix = pitch_matrix(NY, CY).T
    half = NY // 2
    near, far = matrix[:half, :half], matrix[half:, :half]
    assert np.allclose(near, matrix[half:, half:]) and np.allclose(far, matrix[:half, half:])
    stacked = np.concatenate([np.kron(np.eye(2), near), np.kron(np.eye(2), far)], 0)
    return np.concatenate(high_low(stacked), 1)


MATRIX_X = compact_matrix(CX, HALO)
EDGE = HALO - 1
OUTERMOST = float(MATRIX_X[0, 0] / MATRIX_X[0, 1])
assert np.allclose(MATRIX_X[:, 0], OUTERMOST * MATRIX_X[:, 1], rtol=1e-9, atol=1e-12)
SEGMENT = CX + 2 * EDGE
MATRIX_E = MATRIX_X[:, 1:-1]


def split(value):
    high = value.astype(jnp.bfloat16)
    return high, (value - high.astype(jnp.float32)).astype(jnp.bfloat16)


def compact_rows(segment):
    half, end = SEGMENT // 2, SEGMENT - 1
    even = [segment[i] + segment[end - i] for i in range(half)]
    odd = [segment[i] - segment[end - i] for i in range(half)]
    result = [None] * CX
    for i in range(CX // 2):
        row = MATRIX_E[i]
        both = sum(float(0.5 * (row[j] - row[end - j])) * odd[j] for j in range(half))
        diff = sum(float(0.5 * (row[j] + row[end - j])) * even[j] for j in range(half))
        result[i] = both + diff
        result[CX - 1 - i] = both - diff
    return result


def exchange_halves(top, bottom, low_lanes):
    moved = pltpu.roll(jnp.where(low_lanes, bottom, top), NY // 2, axis=1)
    return jnp.where(low_lanes, top, moved), jnp.where(low_lanes, moved, bottom)


def viscosity(temperature):
    return shear_resistance_reference * jnp.exp(sutherland_power_law * jnp.log(temperature))


RUN = 16
RELAYED = (1, 3, 4)
STEPS = [
    (dx, dy, dc)
    for dc in range(2)
    for dx, dy in ((2, 1), (1, 1), (3, 1), (2, 0), (0, 1), (1, 0), (3, 0))
] + [(0, 0, 1)]


def kernel(
    rho_hbm, mom_hbm, en_hbm, dh_hbm, dl_hbm, yc_hbm, ys_hbm, out_ref, con,
    dh, dl, yc, ys, prim, edges, halo_lo, halo_hi, flux_lo, flux_hi,
    speed_send, speed_recv, state_send, state_recv, cross_send, cross_recv,
    slope_send, slope_recv, slope2_send, slope2_recv, div_send, div_recv,
    grad_x, grad_y, flux_x, keep, pitch_in, span_x, rhs_h, rhs_l, dz_t, span_visc,
    sib_value, sib_send_buf, span_in, span_dy, dz_v2, sib_send_sem, sib_recv_sem,
    load_sem, a2a_send_sem, a2a_recv_sem, halo_send_sem, halo_recv_sem, relay, relay_send_sem, relay_recv_sem,
    word_sem,
):
    gx = lax.axis_index("gx")
    me = lax.axis_index("gy")
    n_gx = lax.axis_size("gx")
    right, left = lax.rem(gx + 1, n_gx), lax.rem(gx + n_gx - 1, n_gx)
    chip_x, chip_y, core = me // 4, lax.rem(me // 2, 2), lax.rem(me, 2)
    partners = [
        lax.rem(chip_x + dx, 4) * 4 + lax.rem(chip_y + dy, 2) * 2 + lax.rem(core + dc, 2)
        for dx, dy, dc in STEPS
    ]

    loads = [
        pltpu.make_async_copy(rho_hbm, con.at[0], load_sem.at[0]),
        pltpu.make_async_copy(mom_hbm, con.at[pl.ds(1, 3)], load_sem.at[1]),
        pltpu.make_async_copy(en_hbm, con.at[4], load_sem.at[2]),
        pltpu.make_async_copy(yc_hbm, yc, load_sem.at[3]),
        pltpu.make_async_copy(dh_hbm, dh, load_sem.at[4]),
        pltpu.make_async_copy(dl_hbm, dl, load_sem.at[5]),
        pltpu.make_async_copy(ys_hbm, ys, load_sem.at[6]),
    ]
    for copy in loads:
        copy.start()

    barrier = pltpu.get_barrier_semaphore()
    sibling = partners[-1]
    for (_, _, dc), partner in zip(STEPS, partners):

        @pl.when(lax.rem(core + dc, 2) == 0)
        def _(partner=partner):
            pl.semaphore_signal(barrier, inc=1, device_id={"gy": partner}, device_id_type=MESH)

    gatherer = me - core + 1

    def greet(neighbour):
        pl.semaphore_signal(
            barrier, inc=1, device_id={"gx": neighbour, "gy": gatherer}, device_id_type=MESH
        )

    for neighbour in (left, right):
        greet(neighbour)

    def pass_word():
        pl.semaphore_signal(word_sem, inc=1, device_id={"gy": sibling}, device_id_type=MESH)

    def hear_word():
        pl.semaphore_wait(word_sem, 1)

    run = lax.rem(gx, RUN)
    first_in_run, last_in_run = run == 0, run == RUN - 1
    relays_up, relays_down = run == 1, run == RUN - 2
    beyond_right, beyond_left = lax.rem(gx + 2, n_gx), lax.rem(gx + n_gx - 2, n_gx)
    for condition, source in ((relays_up, beyond_left), (relays_down, beyond_right)):

        @pl.when(condition)
        def _(source=source):
            greet(source)

    low_lanes = lax.broadcasted_iota(jnp.int32, (HZ, NY), 1) < NY // 2

    def a2a(phase, send, recv, step, partner):
        return pltpu.make_async_remote_copy(
            src_ref=send.at[partner],
            dst_ref=recv.at[me],
            send_sem=a2a_send_sem.at[phase, step],
            recv_sem=a2a_recv_sem.at[phase, step],
            device_id={"gy": partner},
            device_id_type=MESH,
        )

    def a2a_start(phase, send, recv):
        for step, partner in enumerate(partners):
            a2a(phase, send, recv, step, partner).start()
        recv[me] = send[me]

    def a2a_wait_recv(phase, send, recv):
        def body(step, carry):
            a2a(phase, send, recv, step, partners[0]).wait_recv()
            return carry

        lax.fori_loop(0, GY - 1, body, 0)

    def a2a_wait_send(phase, send, recv):
        def body(step, carry):
            a2a(phase, send, recv, step, partners[0]).wait_send()
            return carry

        lax.fori_loop(0, GY - 1, body, 0)

    def halo_pair(lo, hi, slot):
        up = pltpu.make_async_remote_copy(
            src_ref=edges.at[slot, 0], dst_ref=lo,
            send_sem=halo_send_sem.at[0, slot], recv_sem=halo_recv_sem.at[0, slot],
            device_id={"gx": right}, device_id_type=MESH,
        )
        down = pltpu.make_async_remote_copy(
            src_ref=edges.at[slot, 1], dst_ref=hi,
            send_sem=halo_send_sem.at[1, slot], recv_sem=halo_recv_sem.at[1, slot],
            device_id={"gx": left}, device_id_type=MESH,
        )
        return up, down

    def halo_start(pair, slot):
        sides = ((pair[0], last_in_run, beyond_right), (pair[1], first_in_run, beyond_left))
        for side, (copy, at_end, target) in enumerate(sides):
            if slot not in RELAYED:
                copy.start()
                continue

            @pl.when(jnp.logical_not(at_end))
            def _(copy=copy):
                copy.start()

            @pl.when(at_end)
            def _(side=side, target=target):
                pltpu.make_async_remote_copy(
                    src_ref=edges.at[slot, side], dst_ref=relay.at[RELAYED.index(slot)],
                    send_sem=halo_send_sem.at[side, slot],
                    recv_sem=relay_recv_sem.at[RELAYED.index(slot)],
                    device_id={"gx": target}, device_id_type=MESH,
                ).start()

    def relay_copies(slot, lo, hi):
        index = RELAYED.index(slot)
        return [
            (
                condition,
                pltpu.make_async_remote_copy(
                    src_ref=relay.at[index], dst_ref=target,
                    send_sem=relay_send_sem.at[index], recv_sem=halo_recv_sem.at[side, slot],
                    device_id={"gx": neighbour}, device_id_type=MESH,
                ),
                pltpu.make_async_remote_copy(
                    src_ref=relay.at[index], dst_ref=relay.at[index],
                    send_sem=relay_send_sem.at[index], recv_sem=relay_recv_sem.at[index],
                    device_id={"gx": neighbour}, device_id_type=MESH,
                ),
            )
            for side, condition, target, neighbour in (
                (0, relays_up, lo, left),
                (1, relays_down, hi, right),
            )
        ]

    def relay_start(copies):
        for condition, forward, arrival in copies:

            @pl.when(condition)
            def _(forward=forward, arrival=arrival):
                arrival.wait_recv()
                forward.start()

    def edge_store(source, slot):
        edges[slot, 0, 0] = source[CX - 3] + OUTERMOST * source[CX - 4]
        edges[slot, 0, 1] = source[CX - 2]
        edges[slot, 0, 2] = source[CX - 1]
        edges[slot, 1, 0] = source[0]
        edges[slot, 1, 1] = source[1]
        edges[slot, 1, 2] = source[2] + OUTERMOST * source[3]

    def sibling_copy(source, slot):
        return pltpu.make_async_remote_copy(
            src_ref=source, dst_ref=sib_value.at[slot],
            send_sem=sib_send_sem.at[slot], recv_sem=sib_recv_sem.at[slot],
            device_id={"gy": sibling}, device_id_type=MESH,
        )

    def pack(send, slot, x, value):
        p0, p1 = exchange_halves(value[:HZ], value[HZ:], low_lanes)
        send[2 * x, slot] = p0
        send[2 * x + 1, slot] = p1

    def unpack(recv, slot, x):
        top, bottom = exchange_halves(recv[2 * x, slot], recv[2 * x + 1, slot], low_lanes)
        return jnp.concatenate([top, bottom], 0)

    def pitch_store(f, x, value):
        high, low = split(value)
        rows = pl.ds(pl.multiple_of(x * ZB, ZB), ZB)
        pitch_in[f, rows, :NY] = high
        pitch_in[f, rows, NY:] = low

    for copy in loads[:3]:
        copy.wait()

    def first(x, carry):
        density, m1, m2, m3, energy = [con[f, x] for f in range(5)]
        inverse = 1.0 / density
        v1, v2, v3 = m1 * inverse, m2 * inverse, m3 * inverse
        kinetic = 0.5 * (m1 * v1 + m2 * v2 + m3 * v3)
        temperature = (heat_ratio - 1.0) * (energy - kinetic) * inverse
        pack(speed_send, 0, x, v1)
        pack(speed_send, 1, x, v3)
        pack(state_send, 0, x, v2)
        pack(state_send, 1, x, density)
        pack(state_send, 2, x, temperature)
        for f, value in enumerate((v1, v2, v3, temperature)):
            prim[f, x] = value
            pitch_store(f, x, value)
        keep[0, x] = viscosity(temperature)
        return carry

    lax.fori_loop(0, CX, first, 0)

    sources = [prim.at[0], prim.at[1], prim.at[2], prim.at[3], con.at[1]]
    for f in range(5):
        edge_store(sources[f], f)

    at_end = jnp.logical_or(first_in_run, last_in_run)
    halos = [halo_pair(halo_lo.at[f], halo_hi.at[f], f) for f in range(5)]

    @pl.when(core == 0)
    def _():
        pl.semaphore_wait(barrier, GY - 1)
        pass_word()

    @pl.when(core == 1)
    def _():
        hear_word()

    def meet():
        @pl.when(jnp.logical_and(core == 1, at_end))
        def _():
            pl.semaphore_wait(barrier, 6)
            pass_word()

        @pl.when(jnp.logical_and(core == 1, jnp.logical_not(at_end)))
        def _():
            pl.semaphore_wait(barrier, 4)
            pass_word()

        @pl.when(core == 0)
        def _():
            hear_word()

        for f in (2, 0):
            halo_start(halos[f], f)

    @pl.when(jnp.logical_not(first_in_run))
    def _():
        meet()

    a2a_start(0, speed_send, speed_recv)
    a2a_start(1, state_send, state_recv)

    @pl.when(first_in_run)
    def _():
        meet()

    for f in (1, 3, 4):
        halo_start(halos[f], f)

    loads[3].wait()

    def pitch_derivative(f):
        product = jnp.dot(pitch_in[f], yc[...], preferred_element_type=jnp.float32)
        return (product[:, :NY] + product[:, NY:]).reshape(CX, ZB, NY)

    for f in (0, 1, 3):
        grad_y[f] = pitch_derivative(f)

    def stream_derivative(own, lo, hi, emit):
        def body(t, carry):
            rows = pl.ds(pl.multiple_of(t * 8, 8), 8)
            segment = [lo[i, rows] for i in range(EDGE)]
            segment += [own[i, rows] for i in range(CX)]
            segment += [hi[i, rows] for i in range(EDGE)]
            for i, value in enumerate(compact_rows(segment)):
                emit(i, rows, value)
            return carry

        lax.fori_loop(0, ZB // 8, body, 0)

    def halo_wait(copies):
        for copy in copies:
            copy.wait_recv()

    def prim_x(f):
        halo_wait(halos[f])

        def emit(i, rows, value):
            grad_x[f, i, rows] = value

        stream_derivative(sources[f], halo_lo.at[f], halo_hi.at[f], emit)

    def cross():
        prim_x(2)
        prim_x(0)

        def extras(x, carry):
            pack(cross_send, 0, x, grad_x[2, x])
            pack(cross_send, 1, x, grad_x[0, x])
            return carry

        lax.fori_loop(0, CX, extras, 0)
        a2a_start(2, cross_send, cross_recv)

    cross()

    relays = [relay_copies(f, halo_lo.at[f], halo_hi.at[f]) for f in (1, 3, 4)]
    for copies in relays:
        relay_start(copies)

    def build(fields):
        def body(s, carry):
            after = lax.rem(s + 1, GY)
            near_rows = pl.ds(pl.multiple_of(s * HZ, HZ), HZ)
            far_rows = pl.ds(pl.multiple_of(NZ // 2 + s * HZ, HZ), HZ)
            for column, fetch in fields:
                columns = pl.ds(column * NY, NY)
                here = fetch(s)
                other = pltpu.roll(jnp.where(low_lanes, fetch(after), here), NY // 2, axis=1)
                high, low = split(here)
                rhs_h[near_rows, columns] = high
                rhs_l[near_rows, columns] = low
                high, low = split(other)
                rhs_h[far_rows, columns] = high
                rhs_l[far_rows, columns] = low
            return carry

        lax.fori_loop(0, GY, body, 0, unroll=2)

    def span_product(start, count):
        columns = pl.ds(start * NY, count * NY)
        high = rhs_h[:, columns]
        product = jnp.dot(dh[...], high, preferred_element_type=jnp.float32)
        product += jnp.dot(dh[...], rhs_l[:, columns], preferred_element_type=jnp.float32)
        product += jnp.dot(dl[...], high, preferred_element_type=jnp.float32)
        return [
            product[:, f * NY : (f + 1) * NY].reshape(GY, HZ, NY) for f in range(count)
        ]

    for copy in loads[4:]:
        copy.wait()
    def half_pitch_derivative(fetch, slot):
        def body(s, carry):
            rows = pl.ds(pl.multiple_of(s * HZ, HZ), HZ)
            for side, value in enumerate((fetch(s), sib_value[slot, s])):
                high, low = split(value)
                span_in[0, rows, side * NY : (side + 1) * NY] = high
                span_in[1, rows, side * NY : (side + 1) * NY] = low
            return carry

        lax.fori_loop(0, GY, body, 0, unroll=2)
        product = jnp.dot(span_in[0], ys[...], preferred_element_type=jnp.float32)
        rest = jnp.dot(span_in[1], ys[:, :NY], preferred_element_type=jnp.float32)
        return (product[:, :NY] + product[:, NY:] + rest).reshape(GY, HZ, NY)

    a2a_wait_recv(0, speed_send, speed_recv)
    siblings = [sibling_copy(speed_recv.at[:, 1], 0), sibling_copy(state_recv.at[:, 0], 1)]
    siblings += [sibling_copy(sib_send_buf.at[f], 2 + f) for f in range(2)]
    siblings[0].start()
    build([(0, lambda s: speed_recv[s, 0]), (1, lambda s: speed_recv[s, 1])])
    for f, value in enumerate(span_product(0, 2)):
        slope_send[:, f] = value
    a2a_start(3, slope_send, slope_recv)

    a2a_wait_recv(1, state_send, state_recv)
    siblings[1].start()

    def span_first(s, carry):
        span_x[0, s] = state_recv[s, 1] * speed_recv[s, 1]
        span_visc[s] = viscosity(state_recv[s, 2])
        return carry

    lax.fori_loop(0, GY, span_first, 0, unroll=2)
    build([(2, lambda s: state_recv[s, 0]), (3, lambda s: span_x[0, s])])
    slopes = span_product(2, 2)
    dz_v2[...] = slopes[0]
    slope2_send[:, 0] = slopes[1]
    a2a_start(4, slope2_send, slope2_recv)

    siblings[0].wait_recv()
    span_dy[0] = half_pitch_derivative(lambda s: speed_recv[s, 1], 0)

    def shear(s, carry):
        s23 = span_visc[s] * (dz_v2[s] + span_dy[0, s])
        sib_send_buf[0, s] = s23
        sib_send_buf[1, s] = s23 * speed_recv[s, 1]
        return carry

    lax.fori_loop(0, GY, shear, 0, unroll=2)
    for copy in siblings[2:]:
        copy.start()
    siblings[1].wait_recv()
    span_dy[1] = half_pitch_derivative(lambda s: state_recv[s, 0], 1)
    build([(4, lambda s: state_recv[s, 2])])
    dz_t[...] = span_product(4, 1)[0]

    for f in range(2):
        siblings[2 + f].wait_recv()
        span_dy[2 + f] = half_pitch_derivative(lambda s, f=f: sib_send_buf[f, s], 2 + f)

    prim_x(1)
    prim_x(3)

    a2a_wait_recv(2, cross_send, cross_recv)

    def span_second(s, carry):
        v1, v3 = speed_recv[s, 0], speed_recv[s, 1]
        v2, density, temperature = [state_recv[s, f] for f in range(3)]
        m3 = span_x[0, s]
        pressure = temperature * density
        enthalpy = (heat_ratio / (heat_ratio - 1.0)) * pressure + 0.5 * density * (
            v1 * v1 + v2 * v2 + v3 * v3
        )
        dz1, dz3 = slope_send[s, 0], slope_send[s, 1]
        dx3, plane = cross_recv[s, 0], cross_recv[s, 1] + span_dy[1, s]
        visc = span_visc[s]
        s13 = visc * (dz1 + dx3)
        s23 = sib_send_buf[0, s]
        s33 = visc * (2.0 * dz3 - (2.0 / 3.0) * (plane + dz3))
        work = s13 * v1 + s23 * v2 + s33 * v3
        span_x[1, s] = m3 * v1 - s13
        span_x[2, s] = m3 * v2 - s23
        span_x[3, s] = m3 * v3 - s33 + pressure
        span_x[4, s] = enthalpy * v3 - work - (visc * conduction) * dz_t[s]
        return carry

    lax.fori_loop(0, GY, span_second, 0, unroll=2)
    build([(5 + f, lambda s, f=f: span_x[1 + f, s]) for f in range(4)])
    for pair in (0, 2):
        for f, value in enumerate(span_product(5 + pair, 2)):
            div_send[:, pair + f] = value - span_dy[pair + f] if pair else value
    a2a_start(5, div_send, div_recv)

    a2a_wait_recv(3, slope_send, slope_recv)

    def stream_flux(x, carry):
        dz1, dz3 = unpack(slope_recv, 0, x), unpack(slope_recv, 1, x)
        density, m1, m2, m3, energy = [con[f, x] for f in range(5)]
        v1, v2, v3, temperature = [prim[f, x] for f in range(4)]
        pressure = temperature * density
        dx1, dx2, dx3, dxt = [grad_x[f, x] for f in range(4)]
        visc = keep[0, x]
        bulk = (2.0 / 3.0) * (dx1 + grad_y[1, x] + dz3)
        s11 = visc * (2.0 * dx1 - bulk)
        s12 = visc * (dx2 + grad_y[0, x])
        s13 = visc * (dx3 + dz1)
        flux_x[0, x] = m1 * v1 + pressure - s11
        flux_x[1, x] = m2 * v1 - s12
        flux_x[2, x] = m3 * v1 - s13
        work = s11 * v1 + s12 * v2 + s13 * v3
        flux_x[3, x] = (energy + pressure) * v1 - work - (visc * conduction) * dxt
        keep[1, x] = bulk
        keep[2, x] = s12
        return carry

    lax.fori_loop(0, CX, stream_flux, 0)
    flux_halos = [halo_pair(flux_lo.at[f], flux_hi.at[f], 5 + f) for f in range(4)]
    for f in range(4):
        edge_store(flux_x.at[f], 5 + f)
        halo_start(flux_halos[f], 5 + f)

    a2a_wait_recv(4, slope2_send, slope2_recv)

    def pitch_flux(x, carry):
        out_ref[0, x] = unpack(slope2_recv, 0, x)
        density, m1, m2, m3, energy = [con[f, x] for f in range(5)]
        v1, v2, v3, temperature = [prim[f, x] for f in range(4)]
        pressure = temperature * density
        visc, bulk, s12 = [keep[f, x] for f in range(3)]
        s22 = visc * (2.0 * grad_y[1, x] - bulk)
        work = s12 * v1 + s22 * v2
        pitch_store(0, x, m2)
        pitch_store(1, x, m1 * v2 - s12)
        pitch_store(2, x, m2 * v2 + pressure - s22)
        pitch_store(3, x, m3 * v2)
        flux = (energy + pressure) * v2 - work - (visc * conduction) * grad_y[3, x]
        pitch_store(4, x, flux)
        return carry

    lax.fori_loop(0, CX, pitch_flux, 0)
    out_ref[0] += pitch_derivative(0)
    for f in range(1, 5):
        out_ref[f] = pitch_derivative(f)

    def accumulate(f, own, lo, hi):
        def emit(i, rows, value):
            out_ref[f, i, rows] += value

        stream_derivative(own, lo, hi, emit)

    halo_wait(halos[4])
    accumulate(0, con.at[1], halo_lo.at[4], halo_hi.at[4])
    for f in range(4):
        halo_wait(flux_halos[f])
        accumulate(1 + f, flux_x.at[f], flux_lo.at[f], flux_hi.at[f])

    a2a_wait_recv(5, div_send, div_recv)

    def last(x, carry):
        for f in range(4):
            out_ref[1 + f, x] += unpack(div_recv, f, x)
        return carry

    lax.fori_loop(0, CX, last, 0)

    a2a_wait_send(0, speed_send, speed_recv)
    a2a_wait_send(1, state_send, state_recv)
    a2a_wait_send(2, cross_send, cross_recv)
    a2a_wait_send(3, slope_send, slope_recv)
    a2a_wait_send(4, slope2_send, slope2_recv)
    a2a_wait_send(5, div_send, div_recv)
    for copy in siblings:
        copy.wait_send()
    for copies in relays:
        for condition, forward, _ in copies:

            @pl.when(condition)
            def _(forward=forward):
                forward.wait_send()

    for copies in halos + flux_halos:
        for copy in copies:
            copy.wait_send()


def per_device(mass_per_volume, momentum, energy):
    dh, dl = span_operand()
    yc = pitch_operand()
    f32, bf16 = jnp.float32, jnp.bfloat16
    field = (CX, ZB, NY)
    piece = (HZ, NY)
    spread, conserved = pl.pallas_call(
        kernel,
        out_shape=[jax.ShapeDtypeStruct((5,) + field, f32)] * 2,
        in_specs=[pl.BlockSpec(memory_space=pltpu.HBM)] * 7,
        out_specs=[pl.BlockSpec(memory_space=pltpu.VMEM)] * 2,
        scratch_shapes=[
            pltpu.VMEM((NZ // 2, NZ), bf16),
            pltpu.VMEM((NZ // 2, NZ), bf16),
            pltpu.VMEM((2 * NY, 2 * NY), bf16),
            pltpu.VMEM((2 * NY, 2 * NY), bf16),
            pltpu.VMEM((4,) + field, f32),
            pltpu.VMEM((9, 2, EDGE, ZB, NY), f32),
            pltpu.VMEM((5, EDGE, ZB, NY), f32),
            pltpu.VMEM((5, EDGE, ZB, NY), f32),
            pltpu.VMEM((4, EDGE, ZB, NY), f32),
            pltpu.VMEM((4, EDGE, ZB, NY), f32),
        ]
        + [pltpu.VMEM((GY, n) + piece, f32) for n in (2, 3, 2, 2, 1, 4) for _ in range(2)]
        + [
            pltpu.VMEM((4,) + field, f32),
            pltpu.VMEM((4,) + field, f32),
            pltpu.VMEM((4,) + field, f32),
            pltpu.VMEM((3,) + field, f32),
            pltpu.VMEM((5, CX * ZB, 2 * NY), bf16),
            pltpu.VMEM((5, GY) + piece, f32),
            pltpu.VMEM((NZ, 9 * NY), bf16),
            pltpu.VMEM((NZ, 9 * NY), bf16),
            pltpu.VMEM((GY,) + piece, f32),
            pltpu.VMEM((GY,) + piece, f32),
            pltpu.VMEM((4, GY) + piece, f32),
            pltpu.VMEM((2, GY) + piece, f32),
            pltpu.VMEM((2, NZ // 2, 2 * NY), bf16),
            pltpu.VMEM((4, GY) + piece, f32),
            pltpu.VMEM((GY,) + piece, f32),
            pltpu.SemaphoreType.DMA((4,)),
            pltpu.SemaphoreType.DMA((4,)),
            pltpu.SemaphoreType.DMA((7,)),
            pltpu.SemaphoreType.DMA((6, GY - 1)),
            pltpu.SemaphoreType.DMA((6, GY - 1)),
            pltpu.SemaphoreType.DMA((2, 9)),
            pltpu.SemaphoreType.DMA((2, 9)),
            pltpu.VMEM((len(RELAYED), EDGE, ZB, NY), f32),
            pltpu.SemaphoreType.DMA((len(RELAYED),)),
            pltpu.SemaphoreType.DMA((len(RELAYED),)),
            pltpu.SemaphoreType.REGULAR,
        ],
        compiler_params=pltpu.CompilerParams(
            collective_id=0, has_side_effects=True, vmem_limit_bytes=24 * 1024 * 1024
        ),
    )(*[pltpu.with_memory_space_constraint(x, pltpu.HBM) for x in (mass_per_volume, momentum, energy, jnp.asarray(dh), jnp.asarray(dl), jnp.asarray(yc), jnp.asarray(half_pitch_operand()))])
    tendency = -spread
    return tendency, conserved + section_step * tendency


def solution(mesh):
    in_specs = (P("gx", "gy", None), P(None, "gx", "gy", None), P("gx", "gy", None))
    out_specs = (P(None, "gx", "gy", None), P(None, "gx", "gy", None))
    return jax.shard_map(
        per_device, mesh=mesh, in_specs=in_specs, out_specs=out_specs, check_vma=False
    )
```

```python
import jax
import jax.numpy as jnp
import ml_dtypes
import numpy as np
from jax import lax
from jax.experimental import pallas as pl
from jax.experimental.pallas import tpu as pltpu
from jax.sharding import PartitionSpec as P

CX = 8
CY = 8
NZ = 512
NY = 128
HALO = 4
GY = 16
ZB = NZ // GY
HZ = ZB // 2
MESH = pl.DeviceIdType.MESH

heat_ratio = 1.4
shear_resistance_reference = 0.08
sutherland_power_law = 0.7
prandtl = 0.72
section_step = 0.05
compact_alpha = 1.0 / 3.0
compact_near = 14.0 / 9.0
compact_far = 1.0 / 9.0
conduction = heat_ratio / ((heat_ratio - 1.0) * prandtl)


def tridiagonal_inverse_product(length, stencil):
    solved = np.array(stencil)
    upper_ratio = np.zeros(length)
    for row_index in range(length):
        if row_index == 0:
            pivot_value = 1.0
            solved[row_index] = solved[row_index] / pivot_value
        else:
            pivot_value = 1.0 - compact_alpha * upper_ratio[row_index - 1]
            solved[row_index] = (
                solved[row_index] - compact_alpha * solved[row_index - 1]
            ) / pivot_value
        upper_ratio[row_index] = compact_alpha / pivot_value
    for row_index in range(length - 2, -1, -1):
        solved[row_index] = solved[row_index] - upper_ratio[row_index] * solved[row_index + 1]
    return solved


def compact_matrix(block_size, margin):
    length = block_size + 2 * margin
    stencil = compact_near / 2.0 * (np.eye(length, k=1) - np.eye(length, k=-1))
    stencil = stencil + compact_far / 4.0 * (np.eye(length, k=2) - np.eye(length, k=-2))
    inverse_product = tridiagonal_inverse_product(length, stencil)
    return inverse_product[margin : margin + block_size]


def pitch_matrix(total, block_size):
    matrix = compact_matrix(block_size, HALO)
    result = np.zeros((total, total))
    rows_all = np.arange(total)
    block_start = rows_all // block_size * block_size
    for offset in range(block_size + 2 * HALO):
        columns = (block_start - HALO + offset) % total
        result[rows_all, columns] += matrix[rows_all % block_size, offset]
    return result


def span_kernel(offsets, total):
    angles = np.pi * offsets / total
    signs = np.where(offsets % 2 == 0, 1.0, -1.0)
    zero = offsets % total == 0
    sines = np.where(zero, 1.0, np.sin(angles))
    return np.where(zero, 0.0, np.pi / total * signs * np.cos(angles) / sines)


def high_low(matrix):
    high = matrix.astype(ml_dtypes.bfloat16)
    low = (matrix - high.astype(np.float64)).astype(ml_dtypes.bfloat16)
    return high, low


def span_operand():
    z = (np.arange(GY)[:, None] * ZB + np.arange(HZ)[None, :]).reshape(-1)
    near = span_kernel(z[:, None] - z[None, :], NZ)
    far = span_kernel(z[:, None] - (z[None, :] + HZ), NZ)
    return high_low(np.concatenate([near, far], 1))


def pitch_operand():
    high, low = high_low(pitch_matrix(NY, CY).T)
    top = np.concatenate([high, low], 1)
    bottom = np.concatenate([high, np.zeros_like(low)], 1)
    return np.concatenate([top, bottom], 0)


def half_pitch_operand():
    matrix = pitch_matrix(NY, CY).T
    half = NY // 2
    near, far = matrix[:half, :half], matrix[half:, :half]
    assert np.allclose(near, matrix[half:, half:]) and np.allclose(far, matrix[:half, half:])
    stacked = np.concatenate([np.kron(np.eye(2), near), np.kron(np.eye(2), far)], 0)
    return np.concatenate(high_low(stacked), 1)


MATRIX_X = compact_matrix(CX, HALO)
EDGE = HALO - 1
OUTERMOST = float(MATRIX_X[0, 0] / MATRIX_X[0, 1])
assert np.allclose(MATRIX_X[:, 0], OUTERMOST * MATRIX_X[:, 1], rtol=1e-9, atol=1e-12)
SEGMENT = CX + 2 * EDGE
MATRIX_E = MATRIX_X[:, 1:-1]


def split(value):
    high = value.astype(jnp.bfloat16)
    return high, (value - high.astype(jnp.float32)).astype(jnp.bfloat16)


def compact_rows(segment):
    half, end = SEGMENT // 2, SEGMENT - 1
    even = [segment[i] + segment[end - i] for i in range(half)]
    odd = [segment[i] - segment[end - i] for i in range(half)]
    result = [None] * CX
    for i in range(CX // 2):
        row = MATRIX_E[i]
        both = sum(float(0.5 * (row[j] - row[end - j])) * odd[j] for j in range(half))
        diff = sum(float(0.5 * (row[j] + row[end - j])) * even[j] for j in range(half))
        result[i] = both + diff
        result[CX - 1 - i] = both - diff
    return result


def exchange_halves(top, bottom, low_lanes):
    moved = pltpu.roll(jnp.where(low_lanes, bottom, top), NY // 2, axis=1)
    return jnp.where(low_lanes, top, moved), jnp.where(low_lanes, moved, bottom)


def viscosity(temperature):
    return shear_resistance_reference * jnp.exp(sutherland_power_law * jnp.log(temperature))


RUN = 16
RELAYED = (1, 3, 4)
STEPS = [
    (dx, dy, dc)
    for dc in range(2)
    for dx, dy in ((2, 1), (1, 1), (3, 1), (2, 0), (0, 1), (1, 0), (3, 0))
] + [(0, 0, 1)]


def kernel(
    rho_hbm, mom_hbm, en_hbm, dh_hbm, dl_hbm, yc_hbm, ys_hbm, out_ref, con,
    dh, dl, yc, ys, prim, edges, halo_lo, halo_hi, flux_lo, flux_hi,
    speed_send, speed_recv, state_send, state_recv, cross_send, cross_recv,
    slope_send, slope_recv, slope2_send, slope2_recv, div_send, div_recv,
    grad_x, grad_y, flux_x, keep, pitch_in, span_x, rhs_h, rhs_l, dz_t, span_visc,
    sib_value, sib_send_buf, span_in, span_dy, dz_v2, sib_send_sem, sib_recv_sem,
    load_sem, a2a_send_sem, a2a_recv_sem, halo_send_sem, halo_recv_sem, relay, relay_send_sem, relay_recv_sem,
    word_sem,
):
    gx = lax.axis_index("gx")
    me = lax.axis_index("gy")
    n_gx = lax.axis_size("gx")
    right, left = lax.rem(gx + 1, n_gx), lax.rem(gx + n_gx - 1, n_gx)
    chip_x, chip_y, core = me // 4, lax.rem(me // 2, 2), lax.rem(me, 2)
    partners = [
        lax.rem(chip_x + dx, 4) * 4 + lax.rem(chip_y + dy, 2) * 2 + lax.rem(core + dc, 2)
        for dx, dy, dc in STEPS
    ]

    loads = [
        pltpu.make_async_copy(rho_hbm, con.at[0], load_sem.at[0]),
        pltpu.make_async_copy(mom_hbm, con.at[pl.ds(1, 3)], load_sem.at[1]),
        pltpu.make_async_copy(en_hbm, con.at[4], load_sem.at[2]),
        pltpu.make_async_copy(yc_hbm, yc, load_sem.at[3]),
        pltpu.make_async_copy(dh_hbm, dh, load_sem.at[4]),
        pltpu.make_async_copy(dl_hbm, dl, load_sem.at[5]),
        pltpu.make_async_copy(ys_hbm, ys, load_sem.at[6]),
    ]
    for copy in loads:
        copy.start()

    barrier = pltpu.get_barrier_semaphore()
    sibling = partners[-1]
    for (_, _, dc), partner in zip(STEPS, partners):

        @pl.when(lax.rem(core + dc, 2) == 0)
        def _(partner=partner):
            pl.semaphore_signal(barrier, inc=1, device_id={"gy": partner}, device_id_type=MESH)

    gatherer = me - core + 1

    def greet(neighbour):
        pl.semaphore_signal(
            barrier, inc=1, device_id={"gx": neighbour, "gy": gatherer}, device_id_type=MESH
        )

    for neighbour in (left, right):
        greet(neighbour)

    def pass_word():
        pl.semaphore_signal(word_sem, inc=1, device_id={"gy": sibling}, device_id_type=MESH)

    def hear_word():
        pl.semaphore_wait(word_sem, 1)

    run = lax.rem(gx, RUN)
    first_in_run, last_in_run = run == 0, run == RUN - 1
    relays_up, relays_down = run == 1, run == RUN - 2
    beyond_right, beyond_left = lax.rem(gx + 2, n_gx), lax.rem(gx + n_gx - 2, n_gx)
    for condition, source in ((relays_up, beyond_left), (relays_down, beyond_right)):

        @pl.when(condition)
        def _(source=source):
            greet(source)

    low_lanes = lax.broadcasted_iota(jnp.int32, (HZ, NY), 1) < NY // 2

    def a2a(phase, send, recv, step, partner):
        return pltpu.make_async_remote_copy(
            src_ref=send.at[partner],
            dst_ref=recv.at[me],
            send_sem=a2a_send_sem.at[phase, step],
            recv_sem=a2a_recv_sem.at[phase, step],
            device_id={"gy": partner},
            device_id_type=MESH,
        )

    def a2a_start(phase, send, recv):
        for step, partner in enumerate(partners):
            a2a(phase, send, recv, step, partner).start()
        recv[me] = send[me]

    def a2a_wait_recv(phase, send, recv):
        def body(step, carry):
            a2a(phase, send, recv, step, partners[0]).wait_recv()
            return carry

        lax.fori_loop(0, GY - 1, body, 0)

    def a2a_wait_send(phase, send, recv):
        def body(step, carry):
            a2a(phase, send, recv, step, partners[0]).wait_send()
            return carry

        lax.fori_loop(0, GY - 1, body, 0)

    def halo_pair(lo, hi, slot):
        up = pltpu.make_async_remote_copy(
            src_ref=edges.at[slot, 0], dst_ref=lo,
            send_sem=halo_send_sem.at[0, slot], recv_sem=halo_recv_sem.at[0, slot],
            device_id={"gx": right}, device_id_type=MESH,
        )
        down = pltpu.make_async_remote_copy(
            src_ref=edges.at[slot, 1], dst_ref=hi,
            send_sem=halo_send_sem.at[1, slot], recv_sem=halo_recv_sem.at[1, slot],
            device_id={"gx": left}, device_id_type=MESH,
        )
        return up, down

    def halo_start(pair, slot):
        sides = ((pair[0], last_in_run, beyond_right), (pair[1], first_in_run, beyond_left))
        for side, (copy, at_end, target) in enumerate(sides):
            if slot not in RELAYED:
                copy.start()
                continue

            @pl.when(jnp.logical_not(at_end))
            def _(copy=copy):
                copy.start()

            @pl.when(at_end)
            def _(side=side, target=target):
                pltpu.make_async_remote_copy(
                    src_ref=edges.at[slot, side], dst_ref=relay.at[RELAYED.index(slot)],
                    send_sem=halo_send_sem.at[side, slot],
                    recv_sem=relay_recv_sem.at[RELAYED.index(slot)],
                    device_id={"gx": target}, device_id_type=MESH,
                ).start()

    def relay_copies(slot, lo, hi):
        index = RELAYED.index(slot)
        return [
            (
                condition,
                pltpu.make_async_remote_copy(
                    src_ref=relay.at[index], dst_ref=target,
                    send_sem=relay_send_sem.at[index], recv_sem=halo_recv_sem.at[side, slot],
                    device_id={"gx": neighbour}, device_id_type=MESH,
                ),
                pltpu.make_async_remote_copy(
                    src_ref=relay.at[index], dst_ref=relay.at[index],
                    send_sem=relay_send_sem.at[index], recv_sem=relay_recv_sem.at[index],
                    device_id={"gx": neighbour}, device_id_type=MESH,
                ),
            )
            for side, condition, target, neighbour in (
                (0, relays_up, lo, left),
                (1, relays_down, hi, right),
            )
        ]

    def relay_start(copies):
        for condition, forward, arrival in copies:

            @pl.when(condition)
            def _(forward=forward, arrival=arrival):
                arrival.wait_recv()
                forward.start()

    def edge_store(source, slot):
        edges[slot, 0, 0] = source[CX - 3] + OUTERMOST * source[CX - 4]
        edges[slot, 0, 1] = source[CX - 2]
        edges[slot, 0, 2] = source[CX - 1]
        edges[slot, 1, 0] = source[0]
        edges[slot, 1, 1] = source[1]
        edges[slot, 1, 2] = source[2] + OUTERMOST * source[3]

    def sibling_copy(source, slot):
        return pltpu.make_async_remote_copy(
            src_ref=source, dst_ref=sib_value.at[slot],
            send_sem=sib_send_sem.at[slot], recv_sem=sib_recv_sem.at[slot],
            device_id={"gy": sibling}, device_id_type=MESH,
        )

    def pack(send, slot, x, value):
        p0, p1 = exchange_halves(value[:HZ], value[HZ:], low_lanes)
        send[2 * x, slot] = p0
        send[2 * x + 1, slot] = p1

    def unpack(recv, slot, x):
        top, bottom = exchange_halves(recv[2 * x, slot], recv[2 * x + 1, slot], low_lanes)
        return jnp.concatenate([top, bottom], 0)

    def pitch_store(f, x, value):
        high, low = split(value)
        rows = pl.ds(pl.multiple_of(x * ZB, ZB), ZB)
        pitch_in[f, rows, :NY] = high
        pitch_in[f, rows, NY:] = low

    for copy in loads[:3]:
        copy.wait()

    def first(x, carry):
        density, m1, m2, m3, energy = [con[f, x] for f in range(5)]
        inverse = 1.0 / density
        v1, v2, v3 = m1 * inverse, m2 * inverse, m3 * inverse
        kinetic = 0.5 * (m1 * v1 + m2 * v2 + m3 * v3)
        temperature = (heat_ratio - 1.0) * (energy - kinetic) * inverse
        pack(speed_send, 0, x, v1)
        pack(speed_send, 1, x, v3)
        pack(state_send, 0, x, v2)
        pack(state_send, 1, x, density)
        pack(state_send, 2, x, temperature)
        for f, value in enumerate((v1, v2, v3, temperature)):
            prim[f, x] = value
            pitch_store(f, x, value)
        keep[0, x] = viscosity(temperature)
        return carry

    lax.fori_loop(0, CX, first, 0)

    sources = [prim.at[0], prim.at[1], prim.at[2], prim.at[3], con.at[1]]
    for f in range(5):
        edge_store(sources[f], f)

    at_end = jnp.logical_or(first_in_run, last_in_run)
    halos = [halo_pair(halo_lo.at[f], halo_hi.at[f], f) for f in range(5)]

    @pl.when(core == 0)
    def _():
        pl.semaphore_wait(barrier, GY - 1)
        pass_word()

    @pl.when(core == 1)
    def _():
        hear_word()

    def meet():
        @pl.when(jnp.logical_and(core == 1, at_end))
        def _():
            pl.semaphore_wait(barrier, 6)
            pass_word()

        @pl.when(jnp.logical_and(core == 1, jnp.logical_not(at_end)))
        def _():
            pl.semaphore_wait(barrier, 4)
            pass_word()

        @pl.when(core == 0)
        def _():
            hear_word()

        for f in (2, 0, 1, 3, 4):
            halo_start(halos[f], f)

    @pl.when(jnp.logical_not(first_in_run))
    def _():
        meet()

    a2a_start(0, speed_send, speed_recv)
    a2a_start(1, state_send, state_recv)

    @pl.when(first_in_run)
    def _():
        meet()


    loads[3].wait()

    def pitch_derivative(f):
        product = jnp.dot(pitch_in[f], yc[...], preferred_element_type=jnp.float32)
        return (product[:, :NY] + product[:, NY:]).reshape(CX, ZB, NY)

    for f in (0, 1, 3):
        grad_y[f] = pitch_derivative(f)

    def stream_derivative(own, lo, hi, emit):
        def body(t, carry):
            rows = pl.ds(pl.multiple_of(t * 8, 8), 8)
            segment = [lo[i, rows] for i in range(EDGE)]
            segment += [own[i, rows] for i in range(CX)]
            segment += [hi[i, rows] for i in range(EDGE)]
            for i, value in enumerate(compact_rows(segment)):
                emit(i, rows, value)
            return carry

        lax.fori_loop(0, ZB // 8, body, 0)

    def halo_wait(copies):
        for copy in copies:
            copy.wait_recv()

    def prim_x(f):
        halo_wait(halos[f])

        def emit(i, rows, value):
            grad_x[f, i, rows] = value

        stream_derivative(sources[f], halo_lo.at[f], halo_hi.at[f], emit)

    def cross():
        prim_x(2)
        prim_x(0)

        def extras(x, carry):
            pack(cross_send, 0, x, grad_x[2, x])
            pack(cross_send, 1, x, grad_x[0, x])
            return carry

        lax.fori_loop(0, CX, extras, 0)
        a2a_start(2, cross_send, cross_recv)

    cross()

    relays = [relay_copies(f, halo_lo.at[f], halo_hi.at[f]) for f in (1, 3, 4)]
    for copies in relays:
        relay_start(copies)

    def build(fields):
        def body(s, carry):
            after = lax.rem(s + 1, GY)
            near_rows = pl.ds(pl.multiple_of(s * HZ, HZ), HZ)
            far_rows = pl.ds(pl.multiple_of(NZ // 2 + s * HZ, HZ), HZ)
            for column, fetch in fields:
                columns = pl.ds(column * NY, NY)
                here = fetch(s)
                other = pltpu.roll(jnp.where(low_lanes, fetch(after), here), NY // 2, axis=1)
                high, low = split(here)
                rhs_h[near_rows, columns] = high
                rhs_l[near_rows, columns] = low
                high, low = split(other)
                rhs_h[far_rows, columns] = high
                rhs_l[far_rows, columns] = low
            return carry

        lax.fori_loop(0, GY, body, 0, unroll=2)

    def span_product(start, count):
        columns = pl.ds(start * NY, count * NY)
        high = rhs_h[:, columns]
        product = jnp.dot(dh[...], high, preferred_element_type=jnp.float32)
        product += jnp.dot(dh[...], rhs_l[:, columns], preferred_element_type=jnp.float32)
        product += jnp.dot(dl[...], high, preferred_element_type=jnp.float32)
        return [
            product[:, f * NY : (f + 1) * NY].reshape(GY, HZ, NY) for f in range(count)
        ]

    for copy in loads[4:]:
        copy.wait()
    def half_pitch_derivative(fetch, slot):
        def body(s, carry):
            rows = pl.ds(pl.multiple_of(s * HZ, HZ), HZ)
            for side, value in enumerate((fetch(s), sib_value[slot, s])):
                high, low = split(value)
                span_in[0, rows, side * NY : (side + 1) * NY] = high
                span_in[1, rows, side * NY : (side + 1) * NY] = low
            return carry

        lax.fori_loop(0, GY, body, 0, unroll=2)
        product = jnp.dot(span_in[0], ys[...], preferred_element_type=jnp.float32)
        rest = jnp.dot(span_in[1], ys[:, :NY], preferred_element_type=jnp.float32)
        return (product[:, :NY] + product[:, NY:] + rest).reshape(GY, HZ, NY)

    a2a_wait_recv(0, speed_send, speed_recv)
    siblings = [sibling_copy(speed_recv.at[:, 1], 0), sibling_copy(state_recv.at[:, 0], 1)]
    siblings += [sibling_copy(sib_send_buf.at[f], 2 + f) for f in range(2)]
    siblings[0].start()
    build([(0, lambda s: speed_recv[s, 0]), (1, lambda s: speed_recv[s, 1])])
    for f, value in enumerate(span_product(0, 2)):
        slope_send[:, f] = value
    a2a_start(3, slope_send, slope_recv)

    a2a_wait_recv(1, state_send, state_recv)
    siblings[1].start()

    def span_first(s, carry):
        span_x[0, s] = state_recv[s, 1] * speed_recv[s, 1]
        span_visc[s] = viscosity(state_recv[s, 2])
        return carry

    lax.fori_loop(0, GY, span_first, 0, unroll=2)
    build([(2, lambda s: state_recv[s, 0]), (3, lambda s: span_x[0, s])])
    slopes = span_product(2, 2)
    dz_v2[...] = slopes[0]
    slope2_send[:, 0] = slopes[1]
    a2a_start(4, slope2_send, slope2_recv)

    siblings[0].wait_recv()
    span_dy[0] = half_pitch_derivative(lambda s: speed_recv[s, 1], 0)

    def shear(s, carry):
        s23 = span_visc[s] * (dz_v2[s] + span_dy[0, s])
        sib_send_buf[0, s] = s23
        sib_send_buf[1, s] = s23 * speed_recv[s, 1]
        return carry

    lax.fori_loop(0, GY, shear, 0, unroll=2)
    for copy in siblings[2:]:
        copy.start()
    siblings[1].wait_recv()
    span_dy[1] = half_pitch_derivative(lambda s: state_recv[s, 0], 1)
    build([(4, lambda s: state_recv[s, 2])])
    dz_t[...] = span_product(4, 1)[0]

    for f in range(2):
        siblings[2 + f].wait_recv()
        span_dy[2 + f] = half_pitch_derivative(lambda s, f=f: sib_send_buf[f, s], 2 + f)

    prim_x(1)
    prim_x(3)

    flux_halos = [halo_pair(flux_lo.at[f], flux_hi.at[f], 5 + f) for f in range(4)]
    def stream_part():
        a2a_wait_recv(3, slope_send, slope_recv)

        def stream_flux(x, carry):
            dz1, dz3 = unpack(slope_recv, 0, x), unpack(slope_recv, 1, x)
            density, m1, m2, m3, energy = [con[f, x] for f in range(5)]
            v1, v2, v3, temperature = [prim[f, x] for f in range(4)]
            pressure = temperature * density
            dx1, dx2, dx3, dxt = [grad_x[f, x] for f in range(4)]
            visc = keep[0, x]
            bulk = (2.0 / 3.0) * (dx1 + grad_y[1, x] + dz3)
            s11 = visc * (2.0 * dx1 - bulk)
            s12 = visc * (dx2 + grad_y[0, x])
            s13 = visc * (dx3 + dz1)
            flux_x[0, x] = m1 * v1 + pressure - s11
            flux_x[1, x] = m2 * v1 - s12
            flux_x[2, x] = m3 * v1 - s13
            work = s11 * v1 + s12 * v2 + s13 * v3
            flux_x[3, x] = (energy + pressure) * v1 - work - (visc * conduction) * dxt
            keep[1, x] = bulk
            keep[2, x] = s12
            return carry

        lax.fori_loop(0, CX, stream_flux, 0)
        for f in range(4):
            edge_store(flux_x.at[f], 5 + f)
            halo_start(flux_halos[f], 5 + f)

    flux_early = last_in_run

    @pl.when(flux_early)
    def _():
        stream_part()

    a2a_wait_recv(2, cross_send, cross_recv)

    def span_second(s, carry):
        v1, v3 = speed_recv[s, 0], speed_recv[s, 1]
        v2, density, temperature = [state_recv[s, f] for f in range(3)]
        m3 = span_x[0, s]
        pressure = temperature * density
        enthalpy = (heat_ratio / (heat_ratio - 1.0)) * pressure + 0.5 * density * (
            v1 * v1 + v2 * v2 + v3 * v3
        )
        dz1, dz3 = slope_send[s, 0], slope_send[s, 1]
        dx3, plane = cross_recv[s, 0], cross_recv[s, 1] + span_dy[1, s]
        visc = span_visc[s]
        s13 = visc * (dz1 + dx3)
        s23 = sib_send_buf[0, s]
        s33 = visc * (2.0 * dz3 - (2.0 / 3.0) * (plane + dz3))
        work = s13 * v1 + s23 * v2 + s33 * v3
        span_x[1, s] = m3 * v1 - s13
        span_x[2, s] = m3 * v2 - s23
        span_x[3, s] = m3 * v3 - s33 + pressure
        span_x[4, s] = enthalpy * v3 - work - (visc * conduction) * dz_t[s]
        return carry

    lax.fori_loop(0, GY, span_second, 0, unroll=2)
    build([(5 + f, lambda s, f=f: span_x[1 + f, s]) for f in range(4)])
    for pair in (0, 2):
        for f, value in enumerate(span_product(5 + pair, 2)):
            div_send[:, pair + f] = value - span_dy[pair + f] if pair else value
    a2a_start(5, div_send, div_recv)

    @pl.when(jnp.logical_not(flux_early))
    def _():
        stream_part()

    a2a_wait_recv(4, slope2_send, slope2_recv)

    def pitch_flux(x, carry):
        out_ref[0, x] = unpack(slope2_recv, 0, x)
        density, m1, m2, m3, energy = [con[f, x] for f in range(5)]
        v1, v2, v3, temperature = [prim[f, x] for f in range(4)]
        pressure = temperature * density
        visc, bulk, s12 = [keep[f, x] for f in range(3)]
        s22 = visc * (2.0 * grad_y[1, x] - bulk)
        work = s12 * v1 + s22 * v2
        pitch_store(0, x, m2)
        pitch_store(1, x, m1 * v2 - s12)
        pitch_store(2, x, m2 * v2 + pressure - s22)
        pitch_store(3, x, m3 * v2)
        flux = (energy + pressure) * v2 - work - (visc * conduction) * grad_y[3, x]
        pitch_store(4, x, flux)
        return carry

    lax.fori_loop(0, CX, pitch_flux, 0)
    out_ref[0] += pitch_derivative(0)
    for f in range(1, 5):
        out_ref[f] = pitch_derivative(f)

    def accumulate(f, own, lo, hi):
        def emit(i, rows, value):
            out_ref[f, i, rows] += value

        stream_derivative(own, lo, hi, emit)

    halo_wait(halos[4])
    accumulate(0, con.at[1], halo_lo.at[4], halo_hi.at[4])
    for f in range(4):
        halo_wait(flux_halos[f])
        accumulate(1 + f, flux_x.at[f], flux_lo.at[f], flux_hi.at[f])

    a2a_wait_recv(5, div_send, div_recv)

    def last(x, carry):
        for f in range(4):
            out_ref[1 + f, x] += unpack(div_recv, f, x)
        return carry

    lax.fori_loop(0, CX, last, 0)

    a2a_wait_send(0, speed_send, speed_recv)
    a2a_wait_send(1, state_send, state_recv)
    a2a_wait_send(2, cross_send, cross_recv)
    a2a_wait_send(3, slope_send, slope_recv)
    a2a_wait_send(4, slope2_send, slope2_recv)
    a2a_wait_send(5, div_send, div_recv)
    for copy in siblings:
        copy.wait_send()
    for copies in relays:
        for condition, forward, _ in copies:

            @pl.when(condition)
            def _(forward=forward):
                forward.wait_send()

    for copies in halos + flux_halos:
        for copy in copies:
            copy.wait_send()


def per_device(mass_per_volume, momentum, energy):
    dh, dl = span_operand()
    yc = pitch_operand()
    f32, bf16 = jnp.float32, jnp.bfloat16
    field = (CX, ZB, NY)
    piece = (HZ, NY)
    spread, conserved = pl.pallas_call(
        kernel,
        out_shape=[jax.ShapeDtypeStruct((5,) + field, f32)] * 2,
        in_specs=[pl.BlockSpec(memory_space=pltpu.HBM)] * 7,
        out_specs=[pl.BlockSpec(memory_space=pltpu.VMEM)] * 2,
        scratch_shapes=[
            pltpu.VMEM((NZ // 2, NZ), bf16),
            pltpu.VMEM((NZ // 2, NZ), bf16),
            pltpu.VMEM((2 * NY, 2 * NY), bf16),
            pltpu.VMEM((2 * NY, 2 * NY), bf16),
            pltpu.VMEM((4,) + field, f32),
            pltpu.VMEM((9, 2, EDGE, ZB, NY), f32),
            pltpu.VMEM((5, EDGE, ZB, NY), f32),
            pltpu.VMEM((5, EDGE, ZB, NY), f32),
            pltpu.VMEM((4, EDGE, ZB, NY), f32),
            pltpu.VMEM((4, EDGE, ZB, NY), f32),
        ]
        + [pltpu.VMEM((GY, n) + piece, f32) for n in (2, 3, 2, 2, 1, 4) for _ in range(2)]
        + [
            pltpu.VMEM((4,) + field, f32),
            pltpu.VMEM((4,) + field, f32),
            pltpu.VMEM((4,) + field, f32),
            pltpu.VMEM((3,) + field, f32),
            pltpu.VMEM((5, CX * ZB, 2 * NY), bf16),
            pltpu.VMEM((5, GY) + piece, f32),
            pltpu.VMEM((NZ, 9 * NY), bf16),
            pltpu.VMEM((NZ, 9 * NY), bf16),
            pltpu.VMEM((GY,) + piece, f32),
            pltpu.VMEM((GY,) + piece, f32),
            pltpu.VMEM((4, GY) + piece, f32),
            pltpu.VMEM((2, GY) + piece, f32),
            pltpu.VMEM((2, NZ // 2, 2 * NY), bf16),
            pltpu.VMEM((4, GY) + piece, f32),
            pltpu.VMEM((GY,) + piece, f32),
            pltpu.SemaphoreType.DMA((4,)),
            pltpu.SemaphoreType.DMA((4,)),
            pltpu.SemaphoreType.DMA((7,)),
            pltpu.SemaphoreType.DMA((6, GY - 1)),
            pltpu.SemaphoreType.DMA((6, GY - 1)),
            pltpu.SemaphoreType.DMA((2, 9)),
            pltpu.SemaphoreType.DMA((2, 9)),
            pltpu.VMEM((len(RELAYED), EDGE, ZB, NY), f32),
            pltpu.SemaphoreType.DMA((len(RELAYED),)),
            pltpu.SemaphoreType.DMA((len(RELAYED),)),
            pltpu.SemaphoreType.REGULAR,
        ],
        compiler_params=pltpu.CompilerParams(
            collective_id=0, has_side_effects=True, vmem_limit_bytes=24 * 1024 * 1024
        ),
    )(*[pltpu.with_memory_space_constraint(x, pltpu.HBM) for x in (mass_per_volume, momentum, energy, jnp.asarray(dh), jnp.asarray(dl), jnp.asarray(yc), jnp.asarray(half_pitch_operand()))])
    tendency = -spread
    return tendency, conserved + section_step * tendency


def solution(mesh):
    in_specs = (P("gx", "gy", None), P(None, "gx", "gy", None), P("gx", "gy", None))
    out_specs = (P(None, "gx", "gy", None), P(None, "gx", "gy", None))
    return jax.shard_map(
        per_device, mesh=mesh, in_specs=in_specs, out_specs=out_specs, check_vma=False
    )
```

```python
import jax
import jax.numpy as jnp
import ml_dtypes
import numpy as np
from jax import lax
from jax.experimental import pallas as pl
from jax.experimental.pallas import tpu as pltpu
from jax.sharding import PartitionSpec as P

CX = 8
CY = 8
NZ = 512
NY = 128
HALO = 4
GY = 16
ZB = NZ // GY
HZ = ZB // 2
MESH = pl.DeviceIdType.MESH

heat_ratio = 1.4
shear_resistance_reference = 0.08
sutherland_power_law = 0.7
prandtl = 0.72
section_step = 0.05
compact_alpha = 1.0 / 3.0
compact_near = 14.0 / 9.0
compact_far = 1.0 / 9.0
conduction = heat_ratio / ((heat_ratio - 1.0) * prandtl)


def tridiagonal_inverse_product(length, stencil):
    solved = np.array(stencil)
    upper_ratio = np.zeros(length)
    for row_index in range(length):
        if row_index == 0:
            pivot_value = 1.0
            solved[row_index] = solved[row_index] / pivot_value
        else:
            pivot_value = 1.0 - compact_alpha * upper_ratio[row_index - 1]
            solved[row_index] = (
                solved[row_index] - compact_alpha * solved[row_index - 1]
            ) / pivot_value
        upper_ratio[row_index] = compact_alpha / pivot_value
    for row_index in range(length - 2, -1, -1):
        solved[row_index] = solved[row_index] - upper_ratio[row_index] * solved[row_index + 1]
    return solved


def compact_matrix(block_size, margin):
    length = block_size + 2 * margin
    stencil = compact_near / 2.0 * (np.eye(length, k=1) - np.eye(length, k=-1))
    stencil = stencil + compact_far / 4.0 * (np.eye(length, k=2) - np.eye(length, k=-2))
    inverse_product = tridiagonal_inverse_product(length, stencil)
    return inverse_product[margin : margin + block_size]


def pitch_matrix(total, block_size):
    matrix = compact_matrix(block_size, HALO)
    result = np.zeros((total, total))
    rows_all = np.arange(total)
    block_start = rows_all // block_size * block_size
    for offset in range(block_size + 2 * HALO):
        columns = (block_start - HALO + offset) % total
        result[rows_all, columns] += matrix[rows_all % block_size, offset]
    return result


def span_kernel(offsets, total):
    angles = np.pi * offsets / total
    signs = np.where(offsets % 2 == 0, 1.0, -1.0)
    zero = offsets % total == 0
    sines = np.where(zero, 1.0, np.sin(angles))
    return np.where(zero, 0.0, np.pi / total * signs * np.cos(angles) / sines)


def high_low(matrix):
    high = matrix.astype(ml_dtypes.bfloat16)
    low = (matrix - high.astype(np.float64)).astype(ml_dtypes.bfloat16)
    return high, low


def span_operand():
    z = (np.arange(GY)[:, None] * ZB + np.arange(HZ)[None, :]).reshape(-1)
    near = span_kernel(z[:, None] - z[None, :], NZ)
    far = span_kernel(z[:, None] - (z[None, :] + HZ), NZ)
    return high_low(np.concatenate([near, far], 1))


def pitch_operand():
    high, low = high_low(pitch_matrix(NY, CY).T)
    top = np.concatenate([high, low], 1)
    bottom = np.concatenate([high, np.zeros_like(low)], 1)
    return np.concatenate([top, bottom], 0)


def half_pitch_operand():
    matrix = pitch_matrix(NY, CY).T
    half = NY // 2
    near, far = matrix[:half, :half], matrix[half:, :half]
    assert np.allclose(near, matrix[half:, half:]) and np.allclose(far, matrix[:half, half:])
    stacked = np.concatenate([np.kron(np.eye(2), near), np.kron(np.eye(2), far)], 0)
    return np.concatenate(high_low(stacked), 1)


MATRIX_X = compact_matrix(CX, HALO)
EDGE = HALO - 1
OUTERMOST = float(MATRIX_X[0, 0] / MATRIX_X[0, 1])
assert np.allclose(MATRIX_X[:, 0], OUTERMOST * MATRIX_X[:, 1], rtol=1e-9, atol=1e-12)
SEGMENT = CX + 2 * EDGE
MATRIX_E = MATRIX_X[:, 1:-1]


def split(value):
    high = value.astype(jnp.bfloat16)
    return high, (value - high.astype(jnp.float32)).astype(jnp.bfloat16)


def compact_rows(segment):
    half, end = SEGMENT // 2, SEGMENT - 1
    even = [segment[i] + segment[end - i] for i in range(half)]
    odd = [segment[i] - segment[end - i] for i in range(half)]
    result = [None] * CX
    for i in range(CX // 2):
        row = MATRIX_E[i]
        both = sum(float(0.5 * (row[j] - row[end - j])) * odd[j] for j in range(half))
        diff = sum(float(0.5 * (row[j] + row[end - j])) * even[j] for j in range(half))
        result[i] = both + diff
        result[CX - 1 - i] = both - diff
    return result


def exchange_halves(top, bottom, low_lanes):
    moved = pltpu.roll(jnp.where(low_lanes, bottom, top), NY // 2, axis=1)
    return jnp.where(low_lanes, top, moved), jnp.where(low_lanes, moved, bottom)


def viscosity(temperature):
    return shear_resistance_reference * jnp.exp(sutherland_power_law * jnp.log(temperature))


RUN = 16
RELAYED = (1, 3, 4)
STEPS = [
    (dx, dy, dc)
    for dc in range(2)
    for dx, dy in ((2, 1), (1, 1), (3, 1), (2, 0), (0, 1), (1, 0), (3, 0))
] + [(0, 0, 1)]


def kernel(
    rho_hbm, mom_hbm, en_hbm, dh_hbm, dl_hbm, yc_hbm, ys_hbm, out_ref, con,
    dh, dl, yc, ys, prim, edges, halo_lo, halo_hi, flux_lo, flux_hi,
    speed_send, speed_recv, state_send, state_recv, cross_send, cross_recv,
    slope_send, slope_recv, slope2_send, slope2_recv, div_send, div_recv,
    grad_x, grad_y, flux_x, keep, pitch_in, span_x, rhs_h, rhs_l, dz_t, span_visc,
    sib_value, sib_send_buf, span_in, span_dy, dz_v2, sib_send_sem, sib_recv_sem,
    load_sem, a2a_send_sem, a2a_recv_sem, halo_send_sem, halo_recv_sem, relay, relay_send_sem, relay_recv_sem,
    word_sem,
):
    gx = lax.axis_index("gx")
    me = lax.axis_index("gy")
    n_gx = lax.axis_size("gx")
    right, left = lax.rem(gx + 1, n_gx), lax.rem(gx + n_gx - 1, n_gx)
    chip_x, chip_y, core = me // 4, lax.rem(me // 2, 2), lax.rem(me, 2)
    partners = [
        lax.rem(chip_x + dx, 4) * 4 + lax.rem(chip_y + dy, 2) * 2 + lax.rem(core + dc, 2)
        for dx, dy, dc in STEPS
    ]

    loads = [
        pltpu.make_async_copy(rho_hbm, con.at[0], load_sem.at[0]),
        pltpu.make_async_copy(mom_hbm, con.at[pl.ds(1, 3)], load_sem.at[1]),
        pltpu.make_async_copy(en_hbm, con.at[4], load_sem.at[2]),
        pltpu.make_async_copy(yc_hbm, yc, load_sem.at[3]),
        pltpu.make_async_copy(dh_hbm, dh, load_sem.at[4]),
        pltpu.make_async_copy(dl_hbm, dl, load_sem.at[5]),
        pltpu.make_async_copy(ys_hbm, ys, load_sem.at[6]),
    ]
    for copy in loads:
        copy.start()

    barrier = pltpu.get_barrier_semaphore()
    sibling = partners[-1]
    for (_, _, dc), partner in zip(STEPS, partners):

        @pl.when(lax.rem(core + dc, 2) == 0)
        def _(partner=partner):
            pl.semaphore_signal(barrier, inc=1, device_id={"gy": partner}, device_id_type=MESH)

    gatherer = me - core + 1

    def greet(neighbour):
        pl.semaphore_signal(
            barrier, inc=1, device_id={"gx": neighbour, "gy": gatherer}, device_id_type=MESH
        )

    for neighbour in (left, right):
        greet(neighbour)

    def pass_word():
        pl.semaphore_signal(word_sem, inc=1, device_id={"gy": sibling}, device_id_type=MESH)

    def hear_word():
        pl.semaphore_wait(word_sem, 1)

    run = lax.rem(gx, RUN)
    first_in_run, last_in_run = run == 0, run == RUN - 1
    relays_up, relays_down = run == 1, run == RUN - 2
    beyond_right, beyond_left = lax.rem(gx + 2, n_gx), lax.rem(gx + n_gx - 2, n_gx)
    for condition, source in ((relays_up, beyond_left), (relays_down, beyond_right)):

        @pl.when(condition)
        def _(source=source):
            greet(source)

    low_lanes = lax.broadcasted_iota(jnp.int32, (HZ, NY), 1) < NY // 2

    def a2a(phase, send, recv, step, partner):
        return pltpu.make_async_remote_copy(
            src_ref=send.at[partner],
            dst_ref=recv.at[me],
            send_sem=a2a_send_sem.at[phase, step],
            recv_sem=a2a_recv_sem.at[phase, step],
            device_id={"gy": partner},
            device_id_type=MESH,
        )

    def a2a_start(phase, send, recv):
        for step, partner in enumerate(partners):
            a2a(phase, send, recv, step, partner).start()
        recv[me] = send[me]

    def a2a_wait_recv(phase, send, recv):
        def body(step, carry):
            a2a(phase, send, recv, step, partners[0]).wait_recv()
            return carry

        lax.fori_loop(0, GY - 1, body, 0)

    def a2a_wait_send(phase, send, recv):
        def body(step, carry):
            a2a(phase, send, recv, step, partners[0]).wait_send()
            return carry

        lax.fori_loop(0, GY - 1, body, 0)

    def halo_pair(lo, hi, slot):
        up = pltpu.make_async_remote_copy(
            src_ref=edges.at[slot, 0], dst_ref=lo,
            send_sem=halo_send_sem.at[0, slot], recv_sem=halo_recv_sem.at[0, slot],
            device_id={"gx": right}, device_id_type=MESH,
        )
        down = pltpu.make_async_remote_copy(
            src_ref=edges.at[slot, 1], dst_ref=hi,
            send_sem=halo_send_sem.at[1, slot], recv_sem=halo_recv_sem.at[1, slot],
            device_id={"gx": left}, device_id_type=MESH,
        )
        return up, down

    def halo_start(pair, slot):
        sides = ((pair[0], last_in_run, beyond_right), (pair[1], first_in_run, beyond_left))
        for side, (copy, at_end, target) in enumerate(sides):
            if slot not in RELAYED:
                copy.start()
                continue

            @pl.when(jnp.logical_not(at_end))
            def _(copy=copy):
                copy.start()

            @pl.when(at_end)
            def _(side=side, target=target):
                pltpu.make_async_remote_copy(
                    src_ref=edges.at[slot, side], dst_ref=relay.at[RELAYED.index(slot)],
                    send_sem=halo_send_sem.at[side, slot],
                    recv_sem=relay_recv_sem.at[RELAYED.index(slot)],
                    device_id={"gx": target}, device_id_type=MESH,
                ).start()

    def relay_copies(slot, lo, hi):
        index = RELAYED.index(slot)
        return [
            (
                condition,
                pltpu.make_async_remote_copy(
                    src_ref=relay.at[index], dst_ref=target,
                    send_sem=relay_send_sem.at[index], recv_sem=halo_recv_sem.at[side, slot],
                    device_id={"gx": neighbour}, device_id_type=MESH,
                ),
                pltpu.make_async_remote_copy(
                    src_ref=relay.at[index], dst_ref=relay.at[index],
                    send_sem=relay_send_sem.at[index], recv_sem=relay_recv_sem.at[index],
                    device_id={"gx": neighbour}, device_id_type=MESH,
                ),
            )
            for side, condition, target, neighbour in (
                (0, relays_up, lo, left),
                (1, relays_down, hi, right),
            )
        ]

    def relay_start(copies):
        for condition, forward, arrival in copies:

            @pl.when(condition)
            def _(forward=forward, arrival=arrival):
                arrival.wait_recv()
                forward.start()

    def edge_store(source, slot):
        edges[slot, 0, 0] = source[CX - 3] + OUTERMOST * source[CX - 4]
        edges[slot, 0, 1] = source[CX - 2]
        edges[slot, 0, 2] = source[CX - 1]
        edges[slot, 1, 0] = source[0]
        edges[slot, 1, 1] = source[1]
        edges[slot, 1, 2] = source[2] + OUTERMOST * source[3]

    def sibling_copy(source, slot):
        return pltpu.make_async_remote_copy(
            src_ref=source, dst_ref=sib_value.at[slot],
            send_sem=sib_send_sem.at[slot], recv_sem=sib_recv_sem.at[slot],
            device_id={"gy": sibling}, device_id_type=MESH,
        )

    def pack(send, slot, x, value):
        p0, p1 = exchange_halves(value[:HZ], value[HZ:], low_lanes)
        send[2 * x, slot] = p0
        send[2 * x + 1, slot] = p1

    def unpack(recv, slot, x):
        top, bottom = exchange_halves(recv[2 * x, slot], recv[2 * x + 1, slot], low_lanes)
        return jnp.concatenate([top, bottom], 0)

    def pitch_store(f, x, value):
        high, low = split(value)
        rows = pl.ds(pl.multiple_of(x * ZB, ZB), ZB)
        pitch_in[f, rows, :NY] = high
        pitch_in[f, rows, NY:] = low

    for copy in loads[:3]:
        copy.wait()

    def first(x, carry):
        density, m1, m2, m3, energy = [con[f, x] for f in range(5)]
        inverse = 1.0 / density
        v1, v2, v3 = m1 * inverse, m2 * inverse, m3 * inverse
        kinetic = 0.5 * (m1 * v1 + m2 * v2 + m3 * v3)
        temperature = (heat_ratio - 1.0) * (energy - kinetic) * inverse
        pack(speed_send, 0, x, v1)
        pack(speed_send, 1, x, v3)
        pack(state_send, 0, x, v2)
        pack(state_send, 1, x, density)
        pack(state_send, 2, x, temperature)
        for f, value in enumerate((v1, v2, v3, temperature)):
            prim[f, x] = value
            pitch_store(f, x, value)
        keep[0, x] = viscosity(temperature)
        return carry

    lax.fori_loop(0, CX, first, 0)

    sources = [prim.at[0], prim.at[1], prim.at[2], prim.at[3], con.at[1]]
    for f in range(5):
        edge_store(sources[f], f)

    at_end = jnp.logical_or(first_in_run, last_in_run)
    halos = [halo_pair(halo_lo.at[f], halo_hi.at[f], f) for f in range(5)]

    @pl.when(core == 0)
    def _():
        pl.semaphore_wait(barrier, GY - 1)
        pass_word()

    @pl.when(core == 1)
    def _():
        hear_word()

    def meet():
        @pl.when(jnp.logical_and(core == 1, at_end))
        def _():
            pl.semaphore_wait(barrier, 6)
            pass_word()

        @pl.when(jnp.logical_and(core == 1, jnp.logical_not(at_end)))
        def _():
            pl.semaphore_wait(barrier, 4)
            pass_word()

        @pl.when(core == 0)
        def _():
            hear_word()

        for f in (2, 0, 1, 3, 4):
            halo_start(halos[f], f)

    @pl.when(jnp.logical_not(first_in_run))
    def _():
        meet()

    a2a_start(0, speed_send, speed_recv)
    a2a_start(1, state_send, state_recv)

    @pl.when(first_in_run)
    def _():
        meet()


    loads[3].wait()

    def pitch_derivative(f):
        product = jnp.dot(pitch_in[f], yc[...], preferred_element_type=jnp.float32)
        return (product[:, :NY] + product[:, NY:]).reshape(CX, ZB, NY)

    for f in (0, 1, 3):
        grad_y[f] = pitch_derivative(f)

    def stream_derivative(own, lo, hi, emit):
        def body(t, carry):
            rows = pl.ds(pl.multiple_of(t * 8, 8), 8)
            segment = [lo[i, rows] for i in range(EDGE)]
            segment += [own[i, rows] for i in range(CX)]
            segment += [hi[i, rows] for i in range(EDGE)]
            for i, value in enumerate(compact_rows(segment)):
                emit(i, rows, value)
            return carry

        lax.fori_loop(0, ZB // 8, body, 0)

    def halo_wait(copies):
        for copy in copies:
            copy.wait_recv()

    def prim_x(f):
        halo_wait(halos[f])

        def emit(i, rows, value):
            grad_x[f, i, rows] = value

        stream_derivative(sources[f], halo_lo.at[f], halo_hi.at[f], emit)

    def cross():
        prim_x(2)
        prim_x(0)

        def extras(x, carry):
            pack(cross_send, 0, x, grad_x[2, x])
            pack(cross_send, 1, x, grad_x[0, x])
            return carry

        lax.fori_loop(0, CX, extras, 0)
        a2a_start(2, cross_send, cross_recv)

    cross()

    relays = [relay_copies(f, halo_lo.at[f], halo_hi.at[f]) for f in (1, 3, 4)]
    for copies in relays:
        relay_start(copies)

    def build(fields):
        def body(s, carry):
            after = lax.rem(s + 1, GY)
            near_rows = pl.ds(pl.multiple_of(s * HZ, HZ), HZ)
            far_rows = pl.ds(pl.multiple_of(NZ // 2 + s * HZ, HZ), HZ)
            for column, fetch in fields:
                columns = pl.ds(column * NY, NY)
                here = fetch(s)
                other = pltpu.roll(jnp.where(low_lanes, fetch(after), here), NY // 2, axis=1)
                high, low = split(here)
                rhs_h[near_rows, columns] = high
                rhs_l[near_rows, columns] = low
                high, low = split(other)
                rhs_h[far_rows, columns] = high
                rhs_l[far_rows, columns] = low
            return carry

        lax.fori_loop(0, GY, body, 0, unroll=2)

    def span_product(start, count):
        columns = pl.ds(start * NY, count * NY)
        high = rhs_h[:, columns]
        product = jnp.dot(dh[...], high, preferred_element_type=jnp.float32)
        product += jnp.dot(dh[...], rhs_l[:, columns], preferred_element_type=jnp.float32)
        product += jnp.dot(dl[...], high, preferred_element_type=jnp.float32)
        return [
            product[:, f * NY : (f + 1) * NY].reshape(GY, HZ, NY) for f in range(count)
        ]

    for copy in loads[4:]:
        copy.wait()
    def half_pitch_derivative(fetch, slot):
        def body(s, carry):
            rows = pl.ds(pl.multiple_of(s * HZ, HZ), HZ)
            for side, value in enumerate((fetch(s), sib_value[slot, s])):
                high, low = split(value)
                span_in[0, rows, side * NY : (side + 1) * NY] = high
                span_in[1, rows, side * NY : (side + 1) * NY] = low
            return carry

        lax.fori_loop(0, GY, body, 0, unroll=2)
        product = jnp.dot(span_in[0], ys[...], preferred_element_type=jnp.float32)
        rest = jnp.dot(span_in[1], ys[:, :NY], preferred_element_type=jnp.float32)
        return (product[:, :NY] + product[:, NY:] + rest).reshape(GY, HZ, NY)

    a2a_wait_recv(0, speed_send, speed_recv)
    siblings = [sibling_copy(speed_recv.at[:, 1], 0), sibling_copy(state_recv.at[:, 0], 1)]
    siblings += [sibling_copy(sib_send_buf.at[f], 2 + f) for f in range(2)]
    siblings[0].start()
    build([(0, lambda s: speed_recv[s, 0]), (1, lambda s: speed_recv[s, 1])])
    for f, value in enumerate(span_product(0, 2)):
        slope_send[:, f] = value
    a2a_start(3, slope_send, slope_recv)

    a2a_wait_recv(1, state_send, state_recv)
    siblings[1].start()

    def span_first(s, carry):
        span_x[0, s] = state_recv[s, 1] * speed_recv[s, 1]
        span_visc[s] = viscosity(state_recv[s, 2])
        return carry

    lax.fori_loop(0, GY, span_first, 0, unroll=2)
    build([(2, lambda s: state_recv[s, 0]), (3, lambda s: span_x[0, s])])
    slopes = span_product(2, 2)
    dz_v2[...] = slopes[0]
    slope2_send[:, 0] = slopes[1]
    a2a_start(4, slope2_send, slope2_recv)

    siblings[0].wait_recv()
    span_dy[0] = half_pitch_derivative(lambda s: speed_recv[s, 1], 0)

    def shear(s, carry):
        s23 = span_visc[s] * (dz_v2[s] + span_dy[0, s])
        sib_send_buf[0, s] = s23
        sib_send_buf[1, s] = s23 * speed_recv[s, 1]
        return carry

    lax.fori_loop(0, GY, shear, 0, unroll=2)
    for copy in siblings[2:]:
        copy.start()
    siblings[1].wait_recv()
    span_dy[1] = half_pitch_derivative(lambda s: state_recv[s, 0], 1)
    build([(4, lambda s: state_recv[s, 2])])
    dz_t[...] = span_product(4, 1)[0]

    for f in range(2):
        siblings[2 + f].wait_recv()
        span_dy[2 + f] = half_pitch_derivative(lambda s, f=f: sib_send_buf[f, s], 2 + f)

    prim_x(1)
    prim_x(3)

    flux_halos = [halo_pair(flux_lo.at[f], flux_hi.at[f], 5 + f) for f in range(4)]
    def stream_part():
        a2a_wait_recv(3, slope_send, slope_recv)

        def stream_flux(x, carry):
            dz1, dz3 = unpack(slope_recv, 0, x), unpack(slope_recv, 1, x)
            density, m1, m2, m3, energy = [con[f, x] for f in range(5)]
            v1, v2, v3, temperature = [prim[f, x] for f in range(4)]
            pressure = temperature * density
            dx1, dx2, dx3, dxt = [grad_x[f, x] for f in range(4)]
            visc = keep[0, x]
            bulk = (2.0 / 3.0) * (dx1 + grad_y[1, x] + dz3)
            s11 = visc * (2.0 * dx1 - bulk)
            s12 = visc * (dx2 + grad_y[0, x])
            s13 = visc * (dx3 + dz1)
            flux_x[0, x] = m1 * v1 + pressure - s11
            flux_x[1, x] = m2 * v1 - s12
            flux_x[2, x] = m3 * v1 - s13
            work = s11 * v1 + s12 * v2 + s13 * v3
            flux_x[3, x] = (energy + pressure) * v1 - work - (visc * conduction) * dxt
            keep[1, x] = bulk
            keep[2, x] = s12
            return carry

        lax.fori_loop(0, CX, stream_flux, 0)
        for f in range(4):
            edge_store(flux_x.at[f], 5 + f)
            halo_start(flux_halos[f], 5 + f)

    flux_early = last_in_run

    @pl.when(flux_early)
    def _():
        stream_part()

    a2a_wait_recv(2, cross_send, cross_recv)

    def span_second(s, carry):
        v1, v3 = speed_recv[s, 0], speed_recv[s, 1]
        v2, density, temperature = [state_recv[s, f] for f in range(3)]
        m3 = span_x[0, s]
        pressure = temperature * density
        enthalpy = (heat_ratio / (heat_ratio - 1.0)) * pressure + 0.5 * density * (
            v1 * v1 + v2 * v2 + v3 * v3
        )
        dz1, dz3 = slope_send[s, 0], slope_send[s, 1]
        dx3, plane = cross_recv[s, 0], cross_recv[s, 1] + span_dy[1, s]
        visc = span_visc[s]
        s13 = visc * (dz1 + dx3)
        s23 = sib_send_buf[0, s]
        s33 = visc * (2.0 * dz3 - (2.0 / 3.0) * (plane + dz3))
        work = s13 * v1 + s23 * v2 + s33 * v3
        span_x[1, s] = m3 * v1 - s13
        span_x[2, s] = m3 * v2 - s23
        span_x[3, s] = m3 * v3 - s33 + pressure
        span_x[4, s] = enthalpy * v3 - work - (visc * conduction) * dz_t[s]
        return carry

    lax.fori_loop(0, GY, span_second, 0, unroll=2)
    build([(5 + f, lambda s, f=f: span_x[1 + f, s]) for f in range(4)])
    for pair in (0, 2):
        for f, value in enumerate(span_product(5 + pair, 2)):
            div_send[:, pair + f] = value - span_dy[pair + f] if pair else value
    a2a_start(5, div_send, div_recv)

    @pl.when(jnp.logical_not(flux_early))
    def _():
        stream_part()

    a2a_wait_recv(4, slope2_send, slope2_recv)

    def pitch_flux(x, carry):
        out_ref[0, x] = unpack(slope2_recv, 0, x)
        density, m1, m2, m3, energy = [con[f, x] for f in range(5)]
        v1, v2, v3, temperature = [prim[f, x] for f in range(4)]
        pressure = temperature * density
        visc, bulk, s12 = [keep[f, x] for f in range(3)]
        s22 = visc * (2.0 * grad_y[1, x] - bulk)
        work = s12 * v1 + s22 * v2
        pitch_store(0, x, m2)
        pitch_store(1, x, m1 * v2 - s12)
        pitch_store(2, x, m2 * v2 + pressure - s22)
        pitch_store(3, x, m3 * v2)
        flux = (energy + pressure) * v2 - work - (visc * conduction) * grad_y[3, x]
        pitch_store(4, x, flux)
        return carry

    lax.fori_loop(0, CX, pitch_flux, 0)
    out_ref[0] += pitch_derivative(0)
    for f in range(1, 5):
        out_ref[f] = pitch_derivative(f)

    def accumulate(f, own, lo, hi):
        def emit(i, rows, value):
            out_ref[f, i, rows] += value

        stream_derivative(own, lo, hi, emit)

    halo_wait(halos[4])
    accumulate(0, con.at[1], halo_lo.at[4], halo_hi.at[4])
    def add_span():
        a2a_wait_recv(5, div_send, div_recv)

        def last(x, carry):
            for f in range(4):
                out_ref[1 + f, x] += unpack(div_recv, f, x)
            return carry

        lax.fori_loop(0, CX, last, 0)

    @pl.when(first_in_run)
    def _():
        add_span()

    for f in range(4):
        halo_wait(flux_halos[f])
        accumulate(1 + f, flux_x.at[f], flux_lo.at[f], flux_hi.at[f])

    @pl.when(jnp.logical_not(first_in_run))
    def _():
        add_span()

    a2a_wait_send(0, speed_send, speed_recv)
    a2a_wait_send(1, state_send, state_recv)
    a2a_wait_send(2, cross_send, cross_recv)
    a2a_wait_send(3, slope_send, slope_recv)
    a2a_wait_send(4, slope2_send, slope2_recv)
    a2a_wait_send(5, div_send, div_recv)
    for copy in siblings:
        copy.wait_send()
    for copies in relays:
        for condition, forward, _ in copies:

            @pl.when(condition)
            def _(forward=forward):
                forward.wait_send()

    for copies in halos + flux_halos:
        for copy in copies:
            copy.wait_send()


def per_device(mass_per_volume, momentum, energy):
    dh, dl = span_operand()
    yc = pitch_operand()
    f32, bf16 = jnp.float32, jnp.bfloat16
    field = (CX, ZB, NY)
    piece = (HZ, NY)
    spread, conserved = pl.pallas_call(
        kernel,
        out_shape=[jax.ShapeDtypeStruct((5,) + field, f32)] * 2,
        in_specs=[pl.BlockSpec(memory_space=pltpu.HBM)] * 7,
        out_specs=[pl.BlockSpec(memory_space=pltpu.VMEM)] * 2,
        scratch_shapes=[
            pltpu.VMEM((NZ // 2, NZ), bf16),
            pltpu.VMEM((NZ // 2, NZ), bf16),
            pltpu.VMEM((2 * NY, 2 * NY), bf16),
            pltpu.VMEM((2 * NY, 2 * NY), bf16),
            pltpu.VMEM((4,) + field, f32),
            pltpu.VMEM((9, 2, EDGE, ZB, NY), f32),
            pltpu.VMEM((5, EDGE, ZB, NY), f32),
            pltpu.VMEM((5, EDGE, ZB, NY), f32),
            pltpu.VMEM((4, EDGE, ZB, NY), f32),
            pltpu.VMEM((4, EDGE, ZB, NY), f32),
        ]
        + [pltpu.VMEM((GY, n) + piece, f32) for n in (2, 3, 2, 2, 1, 4) for _ in range(2)]
        + [
            pltpu.VMEM((4,) + field, f32),
            pltpu.VMEM((4,) + field, f32),
            pltpu.VMEM((4,) + field, f32),
            pltpu.VMEM((3,) + field, f32),
            pltpu.VMEM((5, CX * ZB, 2 * NY), bf16),
            pltpu.VMEM((5, GY) + piece, f32),
            pltpu.VMEM((NZ, 9 * NY), bf16),
            pltpu.VMEM((NZ, 9 * NY), bf16),
            pltpu.VMEM((GY,) + piece, f32),
            pltpu.VMEM((GY,) + piece, f32),
            pltpu.VMEM((4, GY) + piece, f32),
            pltpu.VMEM((2, GY) + piece, f32),
            pltpu.VMEM((2, NZ // 2, 2 * NY), bf16),
            pltpu.VMEM((4, GY) + piece, f32),
            pltpu.VMEM((GY,) + piece, f32),
            pltpu.SemaphoreType.DMA((4,)),
            pltpu.SemaphoreType.DMA((4,)),
            pltpu.SemaphoreType.DMA((7,)),
            pltpu.SemaphoreType.DMA((6, GY - 1)),
            pltpu.SemaphoreType.DMA((6, GY - 1)),
            pltpu.SemaphoreType.DMA((2, 9)),
            pltpu.SemaphoreType.DMA((2, 9)),
            pltpu.VMEM((len(RELAYED), EDGE, ZB, NY), f32),
            pltpu.SemaphoreType.DMA((len(RELAYED),)),
            pltpu.SemaphoreType.DMA((len(RELAYED),)),
            pltpu.SemaphoreType.REGULAR,
        ],
        compiler_params=pltpu.CompilerParams(
            collective_id=0, has_side_effects=True, vmem_limit_bytes=24 * 1024 * 1024
        ),
    )(*[pltpu.with_memory_space_constraint(x, pltpu.HBM) for x in (mass_per_volume, momentum, energy, jnp.asarray(dh), jnp.asarray(dl), jnp.asarray(yc), jnp.asarray(half_pitch_operand()))])
    tendency = -spread
    return tendency, conserved + section_step * tendency


def solution(mesh):
    in_specs = (P("gx", "gy", None), P(None, "gx", "gy", None), P("gx", "gy", None))
    out_specs = (P(None, "gx", "gy", None), P(None, "gx", "gy", None))
    return jax.shard_map(
        per_device, mesh=mesh, in_specs=in_specs, out_specs=out_specs, check_vma=False
    )
```
